256 devices in a mesh: tracer: 2 (over core), dev: 128 (over z, y, x).
Axes of the slice: x: 4, y: 4, z: 8, core: 2. Of those that a mesh axis runs over, the one named last changes fastest.
Arguments:
- coeffs: bfloat16 [2, 256, 256, 2047], P('tracer', 'dev'), may hold values from -6 to 6
- bessel: bfloat16 [2, 1536, 512, 256], P('tracer', 'dev'), may hold values from -0.375 to 0.375
- azimuthal_order_slots: int32 [128], replicated, may hold values from 0 to 1524, as said below
Outputs:
- cross: float32 [2, 768, 512, 512], P('tracer', 'dev')
The draws below stay inside these ranges and needn't reach their ends.
Inputs may be any that keep to these rules, and one draw needn't show every extreme that they name: `azimuthal_order_slots`: the 128 values are exactly the multiples k * (12) for k = 0 .. 127, each once, in an order drawn from the seed.
All inputs are finite; a program needn't handle non-finite values.
Results may differ from the reference program's by a relative error of at most 0.008.
Values may be sent and summed in bfloat16 or wider, within the bound.
No kernel may reach another device: no remote copies, remote signals or barrier semaphores. Data moves between devices by JAX's collectives and lax.ppermute only.
A program may use at most 64 MiB of HBM per device.

```python
import jax
import jax.numpy as jnp
from jax import lax

NSIDE = 512
CYCLES = 2047
LMAX = 1536
SHELLS = 256
KMODES = 512
LB = 128
MWIN = 128
DEGREES_DEV = 12
HALF_DEV = 6


def draw_azimuthal_order_slots(key, part):
    stride = LMAX // MWIN
    shuffled = jax.random.permutation(key, jnp.arange(MWIN, dtype=jnp.int32))
    return (shuffled * stride).astype(jnp.int32)


def levels(key, shape, cuts, smallest, top_value):
    level = 1.0
    for axis_at, blocks in cuts:
        steps = jax.random.uniform(jax.random.fold_in(jax.random.fold_in(key, 6), axis_at), (blocks,), jnp.float32, smallest / len(cuts), top_value / len(cuts))
        level = level * jnp.repeat(jnp.exp(steps), shape[axis_at] // blocks).reshape((-1,) + (1,) * (len(shape) - 1 - axis_at))
    return level


def scatter_about(own_key, extent, deviation, reach, split=(), kind=jnp.bfloat16):
    entries = jax.random.normal(own_key, extent, jnp.float32) * deviation
    if len(split) > 0:
        entries = levels(own_key, extent, split, -0.22, 0.18) * entries
    return jnp.clip(entries, min=-reach, max=reach).astype(kind)


def setup_inputs(seed: int = 0) -> dict:
    key_of = jax.random.split(jax.random.key(seed), 4)
    coeffs = scatter_about(key_of[0], (2, SHELLS, 2 * MWIN, CYCLES), 1.0, 6.0, ((0, 2), (1, 128)))
    bessel = scatter_about(key_of[1], (2, LMAX, KMODES, SHELLS), SHELLS ** -0.5, 0.375, ((0, 2), (1, 128)))
    azimuthal_order_slots = draw_azimuthal_order_slots(jax.random.fold_in(key_of[3], 71), 0)
    return dict(coeffs=coeffs, bessel=bessel, azimuthal_order_slots=azimuthal_order_slots)


rescale_limit = 10000000000.0

def cycle_geometry():
    cycle_number = jnp.arange(1, CYCLES + 1, dtype=jnp.float32)
    nside_float = jnp.float32(NSIDE)
    folded = jnp.minimum(cycle_number, 4.0 * nside_float - cycle_number)
    polar_cycle = folded < nside_float
    polar_gap = folded * folded / (3.0 * nside_float * nside_float)
    equator_height = 4.0 / 3.0 - 2.0 * folded / (3.0 * nside_float)
    cycle_height = jnp.where(polar_cycle, 1.0 - polar_gap, equator_height)
    height_gap = jnp.where(polar_cycle, polar_gap, 1.0 - equator_height)
    sine_cycle = jnp.sqrt(height_gap * (1.0 + cycle_height))
    cosine_latitude = jnp.where(cycle_number <= 2.0 * nside_float, cycle_height, -cycle_height)
    pixels = jnp.where(polar_cycle, 4.0 * folded, 4.0 * nside_float)
    weight = jnp.sqrt(jnp.pi * pixels / (3.0 * nside_float * nside_float))
    return (cosine_latitude, sine_cycle, weight)

def legendre_seed(orders, sine_cycle):
    counter = jnp.arange(1, LMAX + 1, dtype=jnp.float32)
    log_terms = jnp.log1p(-0.5 / counter)
    partial_sum = lax.optimization_barrier(jnp.sum(jnp.where(counter[None, :] <= orders[:, None], log_terms[None, :], 0.0), axis=1))
    head = 0.5 * jnp.log((2.0 * orders + 1.0) / (4.0 * jnp.pi)) + 0.5 * partial_sum
    return head[:, None] + orders[:, None] * jnp.log(sine_cycle)[None, :]

def recurrence_step(carried, degree, orders, cosine_latitude, seed_log):
    previous, current, log_scale = carried
    order_col = orders[:, None]
    alpha_coef = jnp.sqrt(jnp.maximum(4.0 * degree * degree - 1.0, 1.0) / jnp.maximum(degree * degree - order_col * order_col, 1.0))
    degree_below = degree - 1.0
    beta_coef = jnp.sqrt(jnp.maximum(degree_below * degree_below - order_col * order_col, 0.0) / jnp.maximum(4.0 * degree_below * degree_below - 1.0, 1.0))
    starting_degree = degree == order_col
    updated = jnp.where(starting_degree, 1.0, alpha_coef * (cosine_latitude[None, :] * current - beta_coef * previous))
    previous = jnp.where(starting_degree, 0.0, current)
    log_scale = jnp.where(starting_degree, seed_log, log_scale)
    table_value = jnp.where(degree >= order_col, updated * jnp.exp(log_scale), 0.0)
    largest = jnp.maximum(jnp.abs(updated), jnp.abs(previous))
    oversized = largest > rescale_limit
    factor = jnp.where(oversized, 1.0 / jnp.maximum(largest, 1.0), 1.0)
    log_scale = log_scale + jnp.where(oversized, jnp.log(jnp.maximum(largest, 1.0)), 0.0)
    return ((previous * factor, updated * factor, log_scale), table_value)

def legendre_block(carried, first_degree, orders, cosine_latitude, seed_log, weight):

    def advance(inner_state, offset):
        degree = (first_degree + offset).astype(jnp.float32)
        return recurrence_step(inner_state, degree, orders, cosine_latitude, seed_log)
    carried, values = lax.scan(advance, carried, jnp.arange(LB, dtype=jnp.int32), unroll=8)
    return (carried, (values * weight[None, None, :]).astype(jnp.bfloat16))

def reference(coeffs, bessel, azimuthal_order_slots):
    cosine_latitude, sine_cycle, weight = cycle_geometry()
    orders = azimuthal_order_slots.astype(jnp.float32)
    seed_log = legendre_seed(orders, sine_cycle)
    window = azimuthal_order_slots.shape[0]
    grouped_coefficients = coeffs.reshape(2, SHELLS, window, 2, CYCLES).astype(jnp.float32)
    zero_rows = jnp.zeros((window, CYCLES), jnp.float32)
    initial = (zero_rows, zero_rows, zero_rows)

    def one_block(carried, block_index):
        carried, weighted_harmonics = legendre_block(carried, block_index * LB, orders, cosine_latitude, seed_log, weight)
        block_terms = jnp.einsum('lkr,tskcr->tkcls', weighted_harmonics.astype(jnp.float32), grouped_coefficients).astype(jnp.bfloat16)
        return (carried, block_terms)
    final_state, blocks = lax.scan(one_block, initial, jnp.arange(LMAX // LB, dtype=jnp.int32))
    harmonic = jnp.transpose(blocks, (1, 0, 4, 2, 3, 5)).reshape(2, LMAX, 2 * window, SHELLS)
    position = jnp.arange(LMAX, dtype=jnp.int32)
    half_index = position // (LMAX // 2)
    within = position % (LMAX // 2)
    degree_list = within // HALF_DEV * DEGREES_DEV + half_index * HALF_DEV + within % HALF_DEV

    def one_degree(degree):
        leading = jnp.dot(harmonic[0, degree], bessel[0, degree].T, preferred_element_type=jnp.float32).astype(jnp.bfloat16)
        trailing = jnp.dot(harmonic[1, degree], bessel[1, degree].T, preferred_element_type=jnp.float32).astype(jnp.bfloat16)
        tally = jnp.sum((azimuthal_order_slots <= degree).astype(jnp.int32))
        factor = 1.0 / jnp.sqrt(2.0 * tally.astype(jnp.float32))
        return jnp.dot(leading.T, trailing, preferred_element_type=jnp.float32) * factor
    cross = lax.map(one_degree, degree_list)
    return cross.reshape(2, LMAX // 2, KMODES, KMODES)
```

```python
import jax
import jax.numpy as jnp
from jax import lax
from jax.experimental import pallas as pl
from jax.experimental.pallas import tpu as pltpu
from jax.sharding import PartitionSpec as P

NSIDE = 512
CYCLES = 2047
LMAX = 1536
STRIDE = 12
HALF = 1024
PLANE = 16
PLANES = 8
OWNERS = 128
TABLE = LMAX + 16
BLOCK_ROWS = 6 * PLANE
STEP_LOG2 = 64.0
STEP_LN_HIGH = 44.359375
STEP_LN_LOW = 0.0020445558364884
BIG = 2.0**32
SHRINK = 2.0**-64


def half_rows(j):
    return BLOCK_ROWS * (PLANES - j)


def table_base(j):
    return sum(2 * half_rows(i) for i in range(j))


TABLE_ROWS = table_base(PLANES)


def order_index(j, place):
    flip = lax.rem(j, 2)
    return PLANE * j + jnp.where(flip == 0, place, PLANE - 1 - place)


def fold_kernel(slots_ref, coef_ref, out_ref):
    x = coef_ref[0]
    row = lax.broadcasted_iota(jnp.int32, (256, 256), 0)
    col = lax.broadcasted_iota(jnp.int32, (256, 256), 1)
    group = row // 16
    j = (row % 16) // 2
    place = jnp.where(j % 2 == 0, group, PLANE - 1 - group)
    wanted = STRIDE * (PLANE * j + place)
    hit = jnp.logical_and(slots_ref[...] == wanted, row % 2 == col % 2)
    pick = jnp.where(hit, 1.0, 0.0).astype(jnp.bfloat16)
    south = x[:, HALF:].astype(jnp.float32)
    lane = lax.broadcasted_iota(jnp.int32, south.shape, 1)
    south = jnp.where(lane < HALF - 1, south, 0.0).astype(jnp.bfloat16)
    north = jnp.dot(pick, x[:, :HALF], preferred_element_type=jnp.float32)
    south = jnp.dot(pick, south, preferred_element_type=jnp.float32).astype(jnp.bfloat16)
    back_row = lax.broadcasted_iota(jnp.int32, (256, 128), 0)
    back_col = lax.broadcasted_iota(jnp.int32, (256, 128), 1)
    back = jnp.where(back_row + back_col == 254, 1.0, 0.0).astype(jnp.bfloat16)
    for b in range(8):
        if b < 7:
            mirrored = jnp.dot(
                south[:, 128 * (6 - b) : 128 * (8 - b)], back, preferred_element_type=jnp.float32
            )
        else:
            mirrored = jnp.dot(south[:, :128], back[128:], preferred_element_type=jnp.float32)
        here = north[:, 128 * b : 128 * (b + 1)]
        even = (here + mirrored).astype(jnp.bfloat16)
        odd = (here - mirrored).astype(jnp.bfloat16)
        out_ref[:, 0, :, 128 * b : 128 * (b + 1)] = even.reshape(16, 16, 128)
        out_ref[:, 0, :, HALF + 128 * b : HALF + 128 * (b + 1)] = odd.reshape(16, 16, 128)


def fold_coefficients(slots_pair, coeffs):
    return pl.pallas_call(
        fold_kernel,
        grid=(2,),
        in_specs=[
            pl.BlockSpec((1, 256), lambda s: (0, 0)),
            pl.BlockSpec((1, 256, 2 * HALF), lambda s: (s, 0, 0)),
        ],
        out_specs=pl.BlockSpec((16, 1, 16, 2 * HALF), lambda s: (0, s, 0, 0)),
        out_shape=jax.ShapeDtypeStruct((16, 2, 16, 2 * HALF), jnp.bfloat16),
        compiler_params=pltpu.CompilerParams(vmem_limit_bytes=40 * 2**20),
        name="fold",
    )(slots_pair, coeffs)


def legendre_kernel(
    start_ref, a_ref, ab_ref, cos_ref, weight_ref, seed_ref, level_ref, out_ref, rows_ref
):
    x = cos_ref[...]
    weight = weight_ref[...]
    zero = jnp.zeros((8, 128), jnp.float32)

    for j in range(PLANES):
        for h in range(2):
            first = table_base(j) + h * half_rows(j)

            def clear(r, carry, first=first):
                rows_ref[pl.ds(pl.multiple_of(8 * (first + r), 8), 8), :] = zero
                return carry

            lax.fori_loop(0, BLOCK_ROWS, clear, 0, unroll=8)

    tracks = PLANES // 2

    def advance(it, state):
        new_state = []
        for t in range(tracks):
            ja, jb = t, PLANES - 1 - t
            prev, cur, level = state[t]
            ka, kb = start_ref[ja], start_ref[jb]
            first_len = OWNERS - ka
            in_a = it < first_len
            d = jnp.where(in_a, ka + it, kb + it - first_len)
            k = jnp.where(in_a, ka, kb)
            j = jnp.where(in_a, ja, jb)
            fresh = d == k
            prev = jnp.where(fresh, 0.0, prev)
            cur = jnp.where(fresh, seed_ref[j], cur)
            level = jnp.where(fresh, level_ref[j], level)
            biggest = jnp.maximum(jnp.abs(prev), jnp.abs(cur))
            over = biggest > BIG
            factor = jnp.where(over, SHRINK, 1.0)
            prev = prev * factor
            cur = cur * factor
            level = level + jnp.where(over, 1.0, 0.0)
            scale = weight * jnp.exp2(level * STEP_LOG2)
            coef = j * TABLE + STRIDE * d
            per_half = jnp.where(in_a, half_rows(ja), half_rows(jb))
            first = jnp.where(in_a, table_base(ja), table_base(jb)) + 6 * (d - PLANE * j)
            for i in range(STRIDE):
                h, within = divmod(i, 6)
                spot = 8 * (first + h * per_half + within)
                rows_ref[pl.ds(pl.multiple_of(spot, 8), 8), :] = cur * scale
                nxt = (a_ref[coef + i] * x) * cur - ab_ref[coef + i] * prev
                prev, cur = cur, nxt
            new_state.append((prev, cur, level))
        return tuple(new_state)

    lax.fori_loop(0, OWNERS + 1, advance, ((zero, zero, zero),) * tracks)

    def pack(block, carry):
        r0 = pl.multiple_of(block * 16, 16)
        for s in range(8):
            v = rows_ref[pl.ds(8 * r0 + s, 16, stride=8), :]
            out_ref[pl.ds(r0, 16), 128 * s : 128 * (s + 1)] = v.astype(jnp.bfloat16)
        return carry

    lax.fori_loop(0, TABLE_ROWS // 16, pack, 0, unroll=2)


def legendre_tables(start, a_tab, ab_tab, cosine, weight, seed, level):
    smem = pl.BlockSpec(memory_space=pltpu.SMEM)
    vmem = pl.BlockSpec(memory_space=pltpu.VMEM)
    return pl.pallas_call(
        legendre_kernel,
        in_specs=[smem, smem, smem, vmem, vmem, vmem, vmem],
        out_specs=vmem,
        out_shape=jax.ShapeDtypeStruct((TABLE_ROWS, HALF), jnp.bfloat16),
        scratch_shapes=[pltpu.VMEM((8 * TABLE_ROWS, 128), jnp.float32)],
        compiler_params=pltpu.CompilerParams(vmem_limit_bytes=56 * 2**20),
        name="legendre",
    )(start, a_tab, ab_tab, cosine, weight, seed, level)


def transform_kernel(table_hbm, x_ref, out_ref, table, picked, wide, sems):
    copies = []
    for j in range(PLANES):
        for h in range(2):
            first = table_base(j) + h * half_rows(j)
            span = pl.ds(first, half_rows(j))
            copy = pltpu.make_async_copy(table_hbm.at[span], table.at[span], sems.at[2 * j + h])
            copy.start()
            copies.append(copy)
    row = lax.broadcasted_iota(jnp.int32, (512, 512), 0)
    col = lax.broadcasted_iota(jnp.int32, (512, 512), 1)
    source = (row % 32) * 16 + (row // 64) * 2 + (row % 64) // 32
    pick = jnp.where(source == col, 1.0, 0.0).astype(jnp.bfloat16)
    picked[...] = jnp.dot(pick, x_ref[...], preferred_element_type=jnp.float32).astype(jnp.bfloat16)
    contract = (((1,), (1,)), ((), ()))
    for q in range(4):
        mine = picked[128 * q : 128 * (q + 1), :]
        both = jnp.concatenate([mine[:, :HALF], mine[:, HALF:]], axis=0)
        ja, jb = 2 * q, 2 * q + 1
        for h in range(2):
            halves = []
            for j in (ja, jb):
                copies[2 * j + h].wait()
                first = table_base(j) + h * half_rows(j)
                got = lax.dot_general(
                    table[first : first + half_rows(j), :],
                    both,
                    contract,
                    preferred_element_type=jnp.float32,
                )
                parity = lax.broadcasted_iota(jnp.int32, (half_rows(j), 128), 0) % 2
                halves.append(jnp.where(parity == 0, got[:, :128], got[:, 128:]))
            shape = (half_rows(jb), 128)
            lane = lax.broadcasted_iota(jnp.int32, shape, 1)
            joined = jnp.where(lane < 64, halves[0][BLOCK_ROWS:], halves[1])
            lane = lax.broadcasted_iota(jnp.int32, (BLOCK_ROWS, 128), 1)
            opening = jnp.where(lane < 64, halves[0][:BLOCK_ROWS], 0.0)
            base = h * 4 * half_rows(0) + q
            if ja:
                gap = BLOCK_ROWS * ja
                wide[pl.ds(base, gap, stride=4), :] = jnp.zeros((gap, 128), jnp.float32)
            wide[pl.ds(base + 4 * BLOCK_ROWS * ja, BLOCK_ROWS, stride=4), :] = opening
            wide[pl.ds(base + 4 * BLOCK_ROWS * jb, half_rows(jb), stride=4), :] = joined
    out_ref[...] = wide[...].astype(jnp.bfloat16)


def transform(table, x):
    rows = 8 * half_rows(0)
    vmem = pl.BlockSpec(memory_space=pltpu.VMEM)
    return pl.pallas_call(
        transform_kernel,
        in_specs=[pl.BlockSpec(memory_space=pl.ANY), vmem],
        out_specs=vmem,
        out_shape=jax.ShapeDtypeStruct((rows, 128), jnp.bfloat16),
        scratch_shapes=[
            pltpu.VMEM((TABLE_ROWS, HALF), jnp.bfloat16),
            pltpu.VMEM((512, 2 * HALF), jnp.bfloat16),
            pltpu.VMEM((rows, 128), jnp.float32),
            pltpu.SemaphoreType.DMA((16,)),
        ],
        compiler_params=pltpu.CompilerParams(vmem_limit_bytes=56 * 2**20),
        name="transform",
    )(table, x)


def cross_kernel(who_ref, harm_ref, own_ref, other_ref, out_ref, wide):
    i = pl.program_id(0)

    @pl.when(i == 0)
    def _():
        wide[...] = harm_ref[...].astype(jnp.float32)

    tracer, owner = who_ref[0], who_ref[1]
    lane = lax.broadcasted_iota(jnp.int32, (16, 128), 1) // 32
    fields = []
    for t in range(2):
        blocks = []
        for q in range(4):
            tiles = [[], [], [], []]
            for zh in range(2):
                turned = []
                for z4 in range(4):
                    source = (t * OWNERS + (4 * zh + z4) * 16) * 24
                    v = wide[pl.ds(source + 4 * i + q, 16, stride=24), :]
                    turned.append(
                        [v] + [pltpu.roll(v, shift=32 * turn, axis=1) for turn in (1, 2, 3)]
                    )
                for hc in range(4):
                    tile = turned[0][(0 - hc) % 4]
                    for z4 in range(1, 4):
                        tile = jnp.where(lane == z4, turned[z4][(z4 - hc) % 4], tile)
                    tiles[hc].append(tile)
            for hc in range(4):
                blocks.append(jnp.concatenate(tiles[hc], axis=1).astype(jnp.bfloat16))
        fields.append(jnp.concatenate(blocks, axis=0))
    own, other = own_ref[0, 0], other_ref[0]
    first = tracer == 0
    basis_lead = jnp.where(first, own, other)
    basis_trail = jnp.where(first, other, own)
    contract = (((1,), (1,)), ((), ()))
    lead = lax.dot_general(basis_lead, fields[0], contract, preferred_element_type=jnp.float32)
    trail = lax.dot_general(fields[1], basis_trail, contract, preferred_element_type=jnp.float32)
    total = jnp.dot(
        lead.astype(jnp.bfloat16), trail.astype(jnp.bfloat16), preferred_element_type=jnp.float32
    )
    tally = jnp.full((1, 512), owner + 1, jnp.int32).astype(jnp.float32)
    out_ref[0, 0] = total * (1.0 / jnp.sqrt(2.0 * tally))


def cross_spectrum(who, harmonic, bessel, partner):
    return pl.pallas_call(
        cross_kernel,
        grid_spec=pltpu.PrefetchScalarGridSpec(
            num_scalar_prefetch=1,
            grid=(6,),
            in_specs=[
                pl.BlockSpec((256 * 24, 128), lambda i, who: (0, 0)),
                pl.BlockSpec((1, 1, 512, 256), lambda i, who: (0, 6 * who[0] + i, 0, 0)),
                pl.BlockSpec((1, 512, 256), lambda i, who: (i, 0, 0)),
            ],
            out_specs=pl.BlockSpec((1, 1, 512, 512), lambda i, who: (0, i, 0, 0)),
            scratch_shapes=[pltpu.VMEM((256 * 24, 128), jnp.float32)],
        ),
        out_shape=jax.ShapeDtypeStruct((1, 6, 512, 512), jnp.float32),
        compiler_params=pltpu.CompilerParams(vmem_limit_bytes=40 * 2**20),
        name="cross",
    )(who, harmonic, bessel, partner)


def cycle_geometry():
    cycle_number = jnp.arange(1, HALF + 1, dtype=jnp.float32)
    nside_float = jnp.float32(NSIDE)
    polar_cycle = cycle_number < nside_float
    polar_gap = cycle_number * cycle_number / (3.0 * nside_float * nside_float)
    equator_height = 4.0 / 3.0 - 2.0 * cycle_number / (3.0 * nside_float)
    cycle_height = jnp.where(polar_cycle, 1.0 - polar_gap, equator_height)
    height_gap = jnp.where(polar_cycle, polar_gap, 1.0 - equator_height)
    sine_cycle = jnp.sqrt(height_gap * (1.0 + cycle_height))
    pixels = jnp.where(polar_cycle, 4.0 * cycle_number, 4.0 * nside_float)
    weight = jnp.sqrt(jnp.pi * pixels / (3.0 * nside_float * nside_float))
    return (cycle_height, sine_cycle, weight)


def legendre_seed(orders, sine_cycle):
    counter = jnp.arange(1, LMAX + 1, dtype=jnp.float32)
    log_terms = jnp.log1p(-0.5 / counter)
    partial_sum = jnp.sum(
        jnp.where(counter[None, :] <= orders[:, None], log_terms[None, :], 0.0), axis=1
    )
    head = 0.5 * jnp.log((2.0 * orders + 1.0) / (4.0 * jnp.pi)) + 0.5 * partial_sum
    return head[:, None] + orders[:, None] * jnp.log(sine_cycle)[None, :]


def recurrence_tables(orders):
    degree = jnp.arange(1, TABLE + 1, dtype=jnp.float32)[None, :]
    order_col = orders[:, None]
    alpha = jnp.sqrt(
        jnp.maximum(4.0 * degree * degree - 1.0, 1.0)
        / jnp.maximum(degree * degree - order_col * order_col, 1.0)
    )
    below = degree - 1.0
    beta = jnp.sqrt(
        jnp.maximum(below * below - order_col * order_col, 0.0)
        / jnp.maximum(4.0 * below * below - 1.0, 1.0)
    )
    return alpha.reshape(-1), (alpha * beta).reshape(-1)


def per_device(coeffs, bessel, azimuthal_order_slots):
    tracer = lax.axis_index("tracer")
    owner = lax.axis_index("dev")
    place = lax.rem(owner, PLANE)
    plane_groups = [[PLANE * z + i for i in range(PLANE)] for z in range(PLANES)]

    away = lax.dynamic_slice_in_dim(bessel[0], (1 - tracer) * 6, 6, 0)
    partner = lax.ppermute(away, "tracer", [(0, 1), (1, 0)])

    slots_pair = jnp.repeat(azimuthal_order_slots, 2)[None, :]
    folded = fold_coefficients(slots_pair, coeffs[0])
    regrouped = lax.all_to_all(
        folded, "dev", split_axis=0, concat_axis=0, tiled=True, axis_index_groups=plane_groups
    )

    start = order_index(jnp.arange(PLANES, dtype=jnp.int32), place)
    orders = (STRIDE * start).astype(jnp.float32)
    cosine, sine, weight = cycle_geometry()
    seed_log = legendre_seed(orders, sine)
    level = jnp.minimum(jnp.floor(seed_log / (STEP_LN_HIGH + STEP_LN_LOW) + 0.5), 0.0)
    seed = jnp.exp((seed_log - level * STEP_LN_HIGH) - level * STEP_LN_LOW)
    a_tab, ab_tab = recurrence_tables(orders)
    table = legendre_tables(
        start,
        a_tab,
        ab_tab,
        cosine.reshape(8, 128),
        weight.reshape(8, 128),
        seed.reshape(8, 8, 128),
        level.reshape(8, 8, 128),
    )

    harmonic = transform(table, regrouped.reshape(512, 2 * HALF))
    by_degree = lax.all_to_all(
        harmonic.reshape(256, 24, 128), ("tracer", "dev"), split_axis=0, concat_axis=0, tiled=True
    )
    who = jnp.stack([tracer, owner]).astype(jnp.int32)
    return cross_spectrum(who, by_degree.reshape(256 * 24, 128), bessel, partner)


def solution(mesh):
    placed = (P("tracer", "dev", None, None), P("tracer", "dev", None, None), P())
    return jax.shard_map(
        per_device,
        mesh=mesh,
        in_specs=placed,
        out_specs=P("tracer", "dev", None, None),
        check_vma=False,
    )
```

```python
import jax
import jax.numpy as jnp
from jax import lax
from jax.experimental import pallas as pl
from jax.experimental.pallas import tpu as pltpu
from jax.sharding import PartitionSpec as P

NSIDE = 512
CYCLES = 2047
LMAX = 1536
STRIDE = 12
HALF = 1024
PLANE = 16
PLANES = 8
OWNERS = 128
TABLE = LMAX + 16
CHAINS = 4
SPREAD = OWNERS // CHAINS
BLOCK_ROWS = 6 * SPREAD
STEP_LOG2 = 64.0
STEP_LN_HIGH = 44.359375
STEP_LN_LOW = 0.0020445558364884
BIG = 2.0**32
SHRINK = 2.0**-64


def half_rows(j):
    return BLOCK_ROWS * (CHAINS - j)


def table_base(j):
    return sum(2 * half_rows(i) for i in range(j))


TABLE_ROWS = table_base(CHAINS)


def order_index(j, place):
    flip = lax.rem(j, 2)
    return SPREAD * j + jnp.where(flip == 0, place, SPREAD - 1 - place)


def fold_kernel(slots_ref, coef_ref, out_ref):
    x = coef_ref[0]
    row = lax.broadcasted_iota(jnp.int32, (256, 256), 0)
    col = lax.broadcasted_iota(jnp.int32, (256, 256), 1)
    member = row // 8
    j = (row % 8) // 2
    place = jnp.where(j % 2 == 0, member, SPREAD - 1 - member)
    wanted = STRIDE * (SPREAD * j + place)
    hit = jnp.logical_and(slots_ref[...] == wanted, row % 2 == col % 2)
    pick = jnp.where(hit, 1.0, 0.0).astype(jnp.bfloat16)
    south = x[:, HALF:].astype(jnp.float32)
    lane = lax.broadcasted_iota(jnp.int32, south.shape, 1)
    south = jnp.where(lane < HALF - 1, south, 0.0).astype(jnp.bfloat16)
    north = jnp.dot(pick, x[:, :HALF], preferred_element_type=jnp.float32)
    south = jnp.dot(pick, south, preferred_element_type=jnp.float32).astype(jnp.bfloat16)
    back_row = lax.broadcasted_iota(jnp.int32, (256, 128), 0)
    back_col = lax.broadcasted_iota(jnp.int32, (256, 128), 1)
    back = jnp.where(back_row + back_col == 254, 1.0, 0.0).astype(jnp.bfloat16)
    for b in range(8):
        if b < 7:
            mirrored = jnp.dot(
                south[:, 128 * (6 - b) : 128 * (8 - b)], back, preferred_element_type=jnp.float32
            )
        else:
            mirrored = jnp.dot(south[:, :128], back[128:], preferred_element_type=jnp.float32)
        here = north[:, 128 * b : 128 * (b + 1)]
        even = (here + mirrored).astype(jnp.bfloat16)
        odd = (here - mirrored).astype(jnp.bfloat16)
        out_ref[:, 0, :, 128 * b : 128 * (b + 1)] = even.reshape(32, 8, 128)
        out_ref[:, 0, :, HALF + 128 * b : HALF + 128 * (b + 1)] = odd.reshape(32, 8, 128)


def fold_coefficients(slots_pair, coeffs):
    return pl.pallas_call(
        fold_kernel,
        grid=(2,),
        in_specs=[
            pl.BlockSpec((1, 256), lambda s: (0, 0)),
            pl.BlockSpec((1, 256, 2 * HALF), lambda s: (s, 0, 0)),
        ],
        out_specs=pl.BlockSpec((32, 1, 8, 2 * HALF), lambda s: (0, s, 0, 0)),
        out_shape=jax.ShapeDtypeStruct((32, 2, 8, 2 * HALF), jnp.bfloat16),
        compiler_params=pltpu.CompilerParams(vmem_limit_bytes=58 * 2**20),
        name="fold",
    )(slots_pair, coeffs)


def legendre_kernel(
    start_ref, a_ref, ab_ref, cos_ref, weight_ref, seed_ref, level_ref, out_ref, rows_ref
):
    x = cos_ref[...]
    weight = weight_ref[...]
    zero = jnp.zeros((8, 128), jnp.float32)

    for j in range(CHAINS):
        for h in range(2):
            first = table_base(j) + h * half_rows(j)

            def clear(r, carry, first=first):
                rows_ref[pl.ds(pl.multiple_of(8 * (first + r), 8), 8), :] = zero
                return carry

            lax.fori_loop(0, BLOCK_ROWS, clear, 0, unroll=8)

    tracks = CHAINS // 2

    def advance(it, state):
        new_state = []
        for t in range(tracks):
            ja, jb = t, CHAINS - 1 - t
            prev, cur, level = state[t]
            ka, kb = start_ref[ja], start_ref[jb]
            first_len = OWNERS - ka
            in_a = it < first_len
            d = jnp.where(in_a, ka + it, kb + it - first_len)
            k = jnp.where(in_a, ka, kb)
            j = jnp.where(in_a, ja, jb)
            fresh = d == k
            prev = jnp.where(fresh, 0.0, prev)
            cur = jnp.where(fresh, seed_ref[j], cur)
            level = jnp.where(fresh, level_ref[j], level)
            biggest = jnp.maximum(jnp.abs(prev), jnp.abs(cur))
            over = biggest > BIG
            factor = jnp.where(over, SHRINK, 1.0)
            prev = prev * factor
            cur = cur * factor
            level = level + jnp.where(over, 1.0, 0.0)
            scale = weight * jnp.exp2(level * STEP_LOG2)
            coef = j * TABLE + STRIDE * d
            per_half = jnp.where(in_a, half_rows(ja), half_rows(jb))
            first = jnp.where(in_a, table_base(ja), table_base(jb)) + 6 * (d - SPREAD * j)
            for i in range(STRIDE):
                h, within = divmod(i, 6)
                spot = 8 * (first + h * per_half + within)
                rows_ref[pl.ds(pl.multiple_of(spot, 8), 8), :] = cur * scale
                nxt = (a_ref[coef + i] * x) * cur - ab_ref[coef + i] * prev
                prev, cur = cur, nxt
            new_state.append((prev, cur, level))
        return tuple(new_state)

    lax.fori_loop(0, OWNERS + 1, advance, ((zero, zero, zero),) * tracks)

    def pack(block, carry):
        r0 = pl.multiple_of(block * 16, 16)
        for s in range(8):
            v = rows_ref[pl.ds(8 * r0 + s, 16, stride=8), :]
            out_ref[s, pl.ds(r0, 16), :] = v.astype(jnp.bfloat16)
        return carry

    lax.fori_loop(0, TABLE_ROWS // 16, pack, 0, unroll=2)


def legendre_tables(start, a_tab, ab_tab, cosine, weight, seed, level):
    smem = pl.BlockSpec(memory_space=pltpu.SMEM)
    vmem = pl.BlockSpec(memory_space=pltpu.VMEM)
    return pl.pallas_call(
        legendre_kernel,
        in_specs=[smem, smem, smem, vmem, vmem, vmem, vmem],
        out_specs=vmem,
        out_shape=jax.ShapeDtypeStruct((8, TABLE_ROWS, 128), jnp.bfloat16),
        scratch_shapes=[pltpu.VMEM((8 * TABLE_ROWS, 128), jnp.float32)],
        compiler_params=pltpu.CompilerParams(vmem_limit_bytes=56 * 2**20),
        name="legendre",
    )(start, a_tab, ab_tab, cosine, weight, seed, level)


def transform_kernel(table_hbm, x_ref, out_hbm, table, picked, wide, packed, sems):
    copies = []
    for h in range(2):
        for j in range(CHAINS):
            span = pl.ds(table_base(j) + h * half_rows(j), half_rows(j))
            copy = pltpu.make_async_copy(
                table_hbm.at[:, span], table.at[:, span], sems.at[CHAINS * h + j]
            )
            copy.start()
            copies.append(copy)
    row = lax.broadcasted_iota(jnp.int32, (256, 256), 0)
    col = lax.broadcasted_iota(jnp.int32, (256, 256), 1)
    shell = row % 32
    source = (shell // 2) * 16 + (shell % 2) * 8 + (row // 64) * 2 + (row % 64) // 32
    pick = jnp.where(source == col, 1.0, 0.0).astype(jnp.bfloat16)
    for t in range(2):
        got = jnp.dot(
            pick, x_ref[256 * t : 256 * (t + 1), :], preferred_element_type=jnp.float32
        ).astype(jnp.bfloat16)
        for j in range(CHAINS):
            mine = got[64 * j : 64 * (j + 1)]
            picked[j, 64 * t : 64 * (t + 1), :] = mine[:, :HALF]
            picked[j, 128 + 64 * t : 128 + 64 * (t + 1), :] = mine[:, HALF:]
    contract = (((1,), (1,)), ((), ()))
    for h in range(2):
        for j in range(CHAINS):
            both = picked[j]
            copies[CHAINS * h + j].wait()
            first = table_base(j) + h * half_rows(j)
            last = first + half_rows(j)
            rows = jnp.concatenate([table[s, first:last, :] for s in range(8)], axis=1)
            got = lax.dot_general(rows, both, contract, preferred_element_type=jnp.float32)
            parity = lax.broadcasted_iota(jnp.int32, (half_rows(j), 128), 0) % 2
            base = h * 4 * half_rows(0) + j
            gap = BLOCK_ROWS * j
            if gap:
                wide[pl.ds(base, gap, stride=4), :] = jnp.zeros((gap, 128), jnp.float32)
            wide[pl.ds(base + 4 * gap, half_rows(j), stride=4), :] = jnp.where(
                parity == 0, got[:, :128], got[:, 128:]
            )
        half = pl.ds(h * 4 * half_rows(0), 4 * half_rows(0))
        packed[half, :] = wide[half, :].astype(jnp.bfloat16)
        copy = pltpu.make_async_copy(packed.at[half], out_hbm.at[half], sems.at[2 * CHAINS + h])
        copy.start()
        copies.append(copy)
    for copy in copies[2 * CHAINS :]:
        copy.wait()


def transform(table, x):
    rows = 8 * half_rows(0)
    vmem = pl.BlockSpec(memory_space=pltpu.VMEM)
    return pl.pallas_call(
        transform_kernel,
        in_specs=[pl.BlockSpec(memory_space=pl.ANY), vmem],
        out_specs=pl.BlockSpec(memory_space=pltpu.HBM),
        out_shape=jax.ShapeDtypeStruct((rows, 128), jnp.bfloat16),
        scratch_shapes=[
            pltpu.VMEM((8, TABLE_ROWS, 128), jnp.bfloat16),
            pltpu.VMEM((CHAINS, 256, HALF), jnp.bfloat16),
            pltpu.VMEM((rows, 128), jnp.float32),
            pltpu.VMEM((rows, 128), jnp.bfloat16),
            pltpu.SemaphoreType.DMA((2 * CHAINS + 2,)),
        ],
        compiler_params=pltpu.CompilerParams(vmem_limit_bytes=54 * 2**20),
        name="transform",
    )(table, x)


def cross_kernel(who_ref, harm_ref, own_ref, other_ref, out_ref, wide):
    i = pl.program_id(0)

    @pl.when(i == 0)
    def _():
        wide[...] = harm_ref[...].astype(jnp.float32)

    tracer, owner = who_ref[0], who_ref[1]
    lane = lax.broadcasted_iota(jnp.int32, (16, 128), 1) // 32
    blocks = [[], []]
    for core in range(2):
        for j in range(CHAINS):
            tiles = [[], [], [], []]
            for zh in range(2):
                turned = []
                for z4 in range(4):
                    source = (core * OWNERS + (4 * zh + z4) * PLANE) * 24
                    v = wide[pl.ds(source + 4 * i + j, PLANE, stride=24), :]
                    turned.append(
                        [v] + [pltpu.roll(v, shift=32 * turn, axis=1) for turn in (1, 2, 3)]
                    )
                for part in range(4):
                    tile = turned[0][(0 - part) % 4]
                    for z4 in range(1, 4):
                        tile = jnp.where(lane == z4, turned[z4][(z4 - part) % 4], tile)
                    tiles[part].append(tile)
            for part in range(4):
                blocks[part // 2].append(
                    jnp.concatenate(tiles[part], axis=1).astype(jnp.bfloat16)
                )
    fields = [jnp.concatenate(rows, axis=0) for rows in blocks]
    own, other = own_ref[0, 0], other_ref[0]
    first = tracer == 0
    basis_lead = jnp.where(first, own, other)
    basis_trail = jnp.where(first, other, own)
    contract = (((1,), (1,)), ((), ()))
    lead = lax.dot_general(basis_lead, fields[0], contract, preferred_element_type=jnp.float32)
    trail = lax.dot_general(fields[1], basis_trail, contract, preferred_element_type=jnp.float32)
    total = jnp.dot(
        lead.astype(jnp.bfloat16), trail.astype(jnp.bfloat16), preferred_element_type=jnp.float32
    )
    tally = jnp.full((1, 512), owner + 1, jnp.int32).astype(jnp.float32)
    out_ref[0, 0] = total * (1.0 / jnp.sqrt(2.0 * tally))


def cross_spectrum(who, harmonic, bessel, partner):
    return pl.pallas_call(
        cross_kernel,
        grid_spec=pltpu.PrefetchScalarGridSpec(
            num_scalar_prefetch=1,
            grid=(6,),
            in_specs=[
                pl.BlockSpec((256 * 24, 128), lambda i, who: (0, 0)),
                pl.BlockSpec((1, 1, 512, 256), lambda i, who: (0, 6 * who[0] + i, 0, 0)),
                pl.BlockSpec((1, 512, 256), lambda i, who: (i, 0, 0)),
            ],
            out_specs=pl.BlockSpec((1, 1, 512, 512), lambda i, who: (0, i, 0, 0)),
            scratch_shapes=[pltpu.VMEM((256 * 24, 128), jnp.float32)],
        ),
        out_shape=jax.ShapeDtypeStruct((1, 6, 512, 512), jnp.float32),
        compiler_params=pltpu.CompilerParams(vmem_limit_bytes=50 * 2**20),
        name="cross",
    )(who, harmonic, bessel, partner)


def cycle_geometry():
    cycle_number = jnp.arange(1, HALF + 1, dtype=jnp.float32)
    nside_float = jnp.float32(NSIDE)
    polar_cycle = cycle_number < nside_float
    polar_gap = cycle_number * cycle_number / (3.0 * nside_float * nside_float)
    equator_height = 4.0 / 3.0 - 2.0 * cycle_number / (3.0 * nside_float)
    cycle_height = jnp.where(polar_cycle, 1.0 - polar_gap, equator_height)
    height_gap = jnp.where(polar_cycle, polar_gap, 1.0 - equator_height)
    sine_cycle = jnp.sqrt(height_gap * (1.0 + cycle_height))
    pixels = jnp.where(polar_cycle, 4.0 * cycle_number, 4.0 * nside_float)
    weight = jnp.sqrt(jnp.pi * pixels / (3.0 * nside_float * nside_float))
    return (cycle_height, sine_cycle, weight)


def legendre_seed(orders, sine_cycle):
    counter = jnp.arange(1, LMAX + 1, dtype=jnp.float32)
    log_terms = jnp.log1p(-0.5 / counter)
    partial_sum = jnp.sum(
        jnp.where(counter[None, :] <= orders[:, None], log_terms[None, :], 0.0), axis=1
    )
    head = 0.5 * jnp.log((2.0 * orders + 1.0) / (4.0 * jnp.pi)) + 0.5 * partial_sum
    return head[:, None] + orders[:, None] * jnp.log(sine_cycle)[None, :]


def recurrence_tables(orders):
    degree = jnp.arange(1, TABLE + 1, dtype=jnp.float32)[None, :]
    order_col = orders[:, None]
    alpha = jnp.sqrt(
        jnp.maximum(4.0 * degree * degree - 1.0, 1.0)
        / jnp.maximum(degree * degree - order_col * order_col, 1.0)
    )
    below = degree - 1.0
    beta = jnp.sqrt(
        jnp.maximum(below * below - order_col * order_col, 0.0)
        / jnp.maximum(4.0 * below * below - 1.0, 1.0)
    )
    return alpha.reshape(-1), (alpha * beta).reshape(-1)


def per_device(coeffs, bessel, azimuthal_order_slots):
    tracer = lax.axis_index("tracer")
    owner = lax.axis_index("dev")
    place = PLANE * tracer + lax.rem(owner, PLANE)
    plane_groups = [
        [OWNERS * t + PLANE * z + i for t in range(2) for i in range(PLANE)] for z in range(PLANES)
    ]

    away = lax.dynamic_slice_in_dim(bessel[0], (1 - tracer) * 6, 6, 0)
    partner = lax.ppermute(away, "tracer", [(0, 1), (1, 0)])

    slots_pair = jnp.repeat(azimuthal_order_slots, 2)[None, :]
    folded = fold_coefficients(slots_pair, coeffs[0])
    regrouped = lax.all_to_all(
        folded,
        ("tracer", "dev"),
        split_axis=0,
        concat_axis=0,
        tiled=True,
        axis_index_groups=plane_groups,
    )

    start = order_index(jnp.arange(CHAINS, dtype=jnp.int32), place)
    orders = (STRIDE * start).astype(jnp.float32)
    cosine, sine, weight = cycle_geometry()
    seed_log = legendre_seed(orders, sine)
    level = jnp.minimum(jnp.floor(seed_log / (STEP_LN_HIGH + STEP_LN_LOW) + 0.5), 0.0)
    seed = jnp.exp((seed_log - level * STEP_LN_HIGH) - level * STEP_LN_LOW)
    a_tab, ab_tab = recurrence_tables(orders)
    table = legendre_tables(
        start,
        a_tab,
        ab_tab,
        cosine.reshape(8, 128),
        weight.reshape(8, 128),
        seed.reshape(CHAINS, 8, 128),
        level.reshape(CHAINS, 8, 128),
    )

    harmonic = transform(table, regrouped.reshape(512, 2 * HALF))
    by_degree = lax.all_to_all(
        harmonic.reshape(256, 24, 128), ("tracer", "dev"), split_axis=0, concat_axis=0, tiled=True
    )
    who = jnp.stack([tracer, owner]).astype(jnp.int32)
    return cross_spectrum(who, by_degree.reshape(256 * 24, 128), bessel, partner)


def solution(mesh):
    placed = (P("tracer", "dev", None, None), P("tracer", "dev", None, None), P())
    return jax.shard_map(
        per_device,
        mesh=mesh,
        in_specs=placed,
        out_specs=P("tracer", "dev", None, None),
        check_vma=False,
    )
```

```python
import jax
import jax.numpy as jnp
from jax import lax
from jax.experimental import pallas as pl
from jax.experimental.pallas import tpu as pltpu
from jax.sharding import PartitionSpec as P

NSIDE = 512
CYCLES = 2047
LMAX = 1536
STRIDE = 12
HALF = 1024
PLANE = 16
PLANES = 8
OWNERS = 128
TABLE = LMAX + 16
CHAINS = 4
SPREAD = OWNERS // CHAINS
BLOCK_ROWS = 6 * SPREAD
STEP_LOG2 = 64.0
STEP_LN_HIGH = 44.359375
STEP_LN_LOW = 0.0020445558364884
BIG = 2.0**32
SHRINK = 2.0**-64


def half_rows(j):
    return BLOCK_ROWS * (CHAINS - j)


def table_base(j):
    return sum(2 * half_rows(i) for i in range(j))


TABLE_ROWS = table_base(CHAINS)


def order_index(j, place):
    flip = lax.rem(j, 2)
    return SPREAD * j + jnp.where(flip == 0, place, SPREAD - 1 - place)


def fold_kernel(slots_ref, coef_ref, out_ref):
    x = coef_ref[0]
    row = lax.broadcasted_iota(jnp.int32, (256, 256), 0)
    col = lax.broadcasted_iota(jnp.int32, (256, 256), 1)
    member = row // 8
    j = (row % 8) // 2
    place = jnp.where(j % 2 == 0, member, SPREAD - 1 - member)
    wanted = STRIDE * (SPREAD * j + place)
    hit = jnp.logical_and(slots_ref[...] == wanted, row % 2 == col % 2)
    pick = jnp.where(hit, 1.0, 0.0).astype(jnp.bfloat16)
    south = x[:, HALF:].astype(jnp.float32)
    lane = lax.broadcasted_iota(jnp.int32, south.shape, 1)
    south = jnp.where(lane < HALF - 1, south, 0.0).astype(jnp.bfloat16)
    north = jnp.dot(pick, x[:, :HALF], preferred_element_type=jnp.float32)
    south = jnp.dot(pick, south, preferred_element_type=jnp.float32).astype(jnp.bfloat16)
    back_row = lax.broadcasted_iota(jnp.int32, (256, 128), 0)
    back_col = lax.broadcasted_iota(jnp.int32, (256, 128), 1)
    back = jnp.where(back_row + back_col == 254, 1.0, 0.0).astype(jnp.bfloat16)
    for b in range(8):
        if b < 7:
            mirrored = jnp.dot(
                south[:, 128 * (6 - b) : 128 * (8 - b)], back, preferred_element_type=jnp.float32
            )
        else:
            mirrored = jnp.dot(south[:, :128], back[128:], preferred_element_type=jnp.float32)
        here = north[:, 128 * b : 128 * (b + 1)]
        even = (here + mirrored).astype(jnp.bfloat16)
        odd = (here - mirrored).astype(jnp.bfloat16)
        out_ref[:, 0, :, 128 * b : 128 * (b + 1)] = even.reshape(32, 8, 128)
        out_ref[:, 0, :, HALF + 128 * b : HALF + 128 * (b + 1)] = odd.reshape(32, 8, 128)


def fold_coefficients(slots_pair, coeffs):
    return pl.pallas_call(
        fold_kernel,
        grid=(2,),
        in_specs=[
            pl.BlockSpec((1, 256), lambda s: (0, 0)),
            pl.BlockSpec((1, 256, 2 * HALF), lambda s: (s, 0, 0)),
        ],
        out_specs=pl.BlockSpec((32, 1, 8, 2 * HALF), lambda s: (0, s, 0, 0)),
        out_shape=pltpu.HBM((32, 2, 8, 2 * HALF), jnp.bfloat16),
        compiler_params=pltpu.CompilerParams(vmem_limit_bytes=16 * 2**20),
        name="fold",
    )(slots_pair, coeffs)


def legendre_kernel(
    start_ref, a_ref, ab_ref, cos_ref, weight_ref, seed_ref, level_ref, out_ref, rows_ref
):
    x = cos_ref[...]
    weight = weight_ref[...]
    zero = jnp.zeros((8, 128), jnp.float32)

    for j in range(CHAINS):
        for h in range(2):
            first = table_base(j) + h * half_rows(j)

            def clear(r, carry, first=first):
                rows_ref[pl.ds(pl.multiple_of(8 * (first + r), 8), 8), :] = zero
                return carry

            lax.fori_loop(0, BLOCK_ROWS, clear, 0, unroll=8)

    tracks = CHAINS // 2

    def advance(it, state):
        new_state = []
        for t in range(tracks):
            ja, jb = t, CHAINS - 1 - t
            prev, cur, level = state[t]
            ka, kb = start_ref[ja], start_ref[jb]
            first_len = OWNERS - ka
            in_a = it < first_len
            d = jnp.where(in_a, ka + it, kb + it - first_len)
            k = jnp.where(in_a, ka, kb)
            j = jnp.where(in_a, ja, jb)
            fresh = d == k
            prev = jnp.where(fresh, 0.0, prev)
            cur = jnp.where(fresh, seed_ref[j], cur)
            level = jnp.where(fresh, level_ref[j], level)
            biggest = jnp.maximum(jnp.abs(prev), jnp.abs(cur))
            over = biggest > BIG
            factor = jnp.where(over, SHRINK, 1.0)
            prev = prev * factor
            cur = cur * factor
            level = level + jnp.where(over, 1.0, 0.0)
            scale = weight * jnp.exp2(level * STEP_LOG2)
            coef = j * TABLE + STRIDE * d
            per_half = jnp.where(in_a, half_rows(ja), half_rows(jb))
            first = jnp.where(in_a, table_base(ja), table_base(jb)) + 6 * (d - SPREAD * j)
            for i in range(STRIDE):
                h, within = divmod(i, 6)
                spot = 8 * (first + h * per_half + within)
                rows_ref[pl.ds(pl.multiple_of(spot, 8), 8), :] = cur * scale
                nxt = (a_ref[coef + i] * x) * cur - ab_ref[coef + i] * prev
                prev, cur = cur, nxt
            new_state.append((prev, cur, level))
        return tuple(new_state)

    lax.fori_loop(0, OWNERS + 1, advance, ((zero, zero, zero),) * tracks)

    def pack(block, carry):
        r0 = pl.multiple_of(block * 16, 16)
        for s in range(8):
            v = rows_ref[pl.ds(8 * r0 + s, 16, stride=8), :]
            out_ref[s, pl.ds(r0, 16), :] = v.astype(jnp.bfloat16)
        return carry

    lax.fori_loop(0, TABLE_ROWS // 16, pack, 0, unroll=2)


def legendre_tables(start, a_tab, ab_tab, cosine, weight, seed, level):
    smem = pl.BlockSpec(memory_space=pltpu.SMEM)
    vmem = pl.BlockSpec(memory_space=pltpu.VMEM)
    return pl.pallas_call(
        legendre_kernel,
        in_specs=[smem, smem, smem, vmem, vmem, vmem, vmem],
        out_specs=vmem,
        out_shape=jax.ShapeDtypeStruct((8, TABLE_ROWS, 128), jnp.bfloat16),
        scratch_shapes=[pltpu.VMEM((8 * TABLE_ROWS, 128), jnp.float32)],
        compiler_params=pltpu.CompilerParams(vmem_limit_bytes=28 * 2**20),
        name="legendre",
    )(start, a_tab, ab_tab, cosine, weight, seed, level)


def transform_kernel(table_hbm, x_ref, out_hbm, table, picked, wide, packed, sems):
    copies = []
    for h in range(2):
        for j in range(CHAINS):
            span = pl.ds(table_base(j) + h * half_rows(j), half_rows(j))
            copy = pltpu.make_async_copy(
                table_hbm.at[:, span], table.at[:, span], sems.at[CHAINS * h + j]
            )
            copy.start()
            copies.append(copy)
    row = lax.broadcasted_iota(jnp.int32, (256, 256), 0)
    col = lax.broadcasted_iota(jnp.int32, (256, 256), 1)
    shell = row % 32
    source = (shell // 2) * 16 + (shell % 2) * 8 + (row // 64) * 2 + (row % 64) // 32
    pick = jnp.where(source == col, 1.0, 0.0).astype(jnp.bfloat16)
    for t in range(2):
        got = jnp.dot(
            pick, x_ref[256 * t : 256 * (t + 1), :], preferred_element_type=jnp.float32
        ).astype(jnp.bfloat16)
        for j in range(CHAINS):
            mine = got[64 * j : 64 * (j + 1)]
            picked[j, 64 * t : 64 * (t + 1), :] = mine[:, :HALF]
            picked[j, 128 + 64 * t : 128 + 64 * (t + 1), :] = mine[:, HALF:]
    contract = (((1,), (1,)), ((), ()))
    for h in range(2):
        for j in range(CHAINS):
            both = picked[j]
            copies[CHAINS * h + j].wait()
            first = table_base(j) + h * half_rows(j)
            last = first + half_rows(j)
            rows = jnp.concatenate([table[s, first:last, :] for s in range(8)], axis=1)
            got = lax.dot_general(rows, both, contract, preferred_element_type=jnp.float32)
            parity = lax.broadcasted_iota(jnp.int32, (half_rows(j), 128), 0) % 2
            base = h * 4 * half_rows(0) + j
            gap = BLOCK_ROWS * j
            if gap:
                wide[pl.ds(base, gap, stride=4), :] = jnp.zeros((gap, 128), jnp.float32)
            wide[pl.ds(base + 4 * gap, half_rows(j), stride=4), :] = jnp.where(
                parity == 0, got[:, :128], got[:, 128:]
            )
        half = pl.ds(h * 4 * half_rows(0), 4 * half_rows(0))
        packed[half, :] = wide[half, :].astype(jnp.bfloat16)
        copy = pltpu.make_async_copy(packed.at[half], out_hbm.at[half], sems.at[2 * CHAINS + h])
        copy.start()
        copies.append(copy)
    for copy in copies[2 * CHAINS :]:
        copy.wait()


def transform(table, x):
    rows = 8 * half_rows(0)
    vmem = pl.BlockSpec(memory_space=pltpu.VMEM)
    return pl.pallas_call(
        transform_kernel,
        in_specs=[pl.BlockSpec(memory_space=pl.ANY), vmem],
        out_specs=pl.BlockSpec(memory_space=pltpu.HBM),
        out_shape=pltpu.HBM((rows, 128), jnp.bfloat16),
        scratch_shapes=[
            pltpu.VMEM((8, TABLE_ROWS, 128), jnp.bfloat16),
            pltpu.VMEM((CHAINS, 256, HALF), jnp.bfloat16),
            pltpu.VMEM((rows, 128), jnp.float32),
            pltpu.VMEM((rows, 128), jnp.bfloat16),
            pltpu.SemaphoreType.DMA((2 * CHAINS + 2,)),
        ],
        compiler_params=pltpu.CompilerParams(vmem_limit_bytes=24 * 2**20),
        name="transform",
    )(pltpu.with_memory_space_constraint(table, pltpu.HBM), x)


def cross_kernel(who_ref, harm_ref, own_ref, other_ref, out_ref, wide):
    i = pl.program_id(0)

    @pl.when(i == 0)
    def _():
        wide[...] = harm_ref[...].astype(jnp.float32)

    tracer, owner = who_ref[0], who_ref[1]
    lane = lax.broadcasted_iota(jnp.int32, (16, 128), 1) // 32
    blocks = [[], []]
    for core in range(2):
        for j in range(CHAINS):
            tiles = [[], [], [], []]
            for zh in range(2):
                turned = []
                for z4 in range(4):
                    source = (core * OWNERS + (4 * zh + z4) * PLANE) * 24
                    v = wide[pl.ds(source + 4 * i + j, PLANE, stride=24), :]
                    turned.append(
                        [v] + [pltpu.roll(v, shift=32 * turn, axis=1) for turn in (1, 2, 3)]
                    )
                for part in range(4):
                    tile = turned[0][(0 - part) % 4]
                    for z4 in range(1, 4):
                        tile = jnp.where(lane == z4, turned[z4][(z4 - part) % 4], tile)
                    tiles[part].append(tile)
            for part in range(4):
                blocks[part // 2].append(
                    jnp.concatenate(tiles[part], axis=1).astype(jnp.bfloat16)
                )
    fields = [jnp.concatenate(rows, axis=0) for rows in blocks]
    own, other = own_ref[0, 0], other_ref[0]
    first = tracer == 0
    basis_lead = jnp.where(first, own, other)
    basis_trail = jnp.where(first, other, own)
    contract = (((1,), (1,)), ((), ()))
    lead = lax.dot_general(basis_lead, fields[0], contract, preferred_element_type=jnp.float32)
    trail = lax.dot_general(fields[1], basis_trail, contract, preferred_element_type=jnp.float32)
    total = jnp.dot(
        lead.astype(jnp.bfloat16), trail.astype(jnp.bfloat16), preferred_element_type=jnp.float32
    )
    tally = jnp.full((1, 512), owner + 1, jnp.int32).astype(jnp.float32)
    out_ref[0, 0] = total * (1.0 / jnp.sqrt(2.0 * tally))


def cross_spectrum(who, harmonic, bessel, partner):
    return pl.pallas_call(
        cross_kernel,
        grid_spec=pltpu.PrefetchScalarGridSpec(
            num_scalar_prefetch=1,
            grid=(6,),
            in_specs=[
                pl.BlockSpec((256 * 24, 128), lambda i, who: (0, 0)),
                pl.BlockSpec((1, 1, 512, 256), lambda i, who: (0, 6 * who[0] + i, 0, 0)),
                pl.BlockSpec((1, 512, 256), lambda i, who: (i, 0, 0)),
            ],
            out_specs=pl.BlockSpec((1, 1, 512, 512), lambda i, who: (0, i, 0, 0)),
            scratch_shapes=[pltpu.VMEM((256 * 24, 128), jnp.float32)],
        ),
        out_shape=jax.ShapeDtypeStruct((1, 6, 512, 512), jnp.float32),
        compiler_params=pltpu.CompilerParams(vmem_limit_bytes=20 * 2**20),
        name="cross",
    )(who, harmonic, bessel, pltpu.with_memory_space_constraint(partner, pltpu.HBM))


def cycle_geometry():
    cycle_number = jnp.arange(1, HALF + 1, dtype=jnp.float32)
    nside_float = jnp.float32(NSIDE)
    polar_cycle = cycle_number < nside_float
    polar_gap = cycle_number * cycle_number / (3.0 * nside_float * nside_float)
    equator_height = 4.0 / 3.0 - 2.0 * cycle_number / (3.0 * nside_float)
    cycle_height = jnp.where(polar_cycle, 1.0 - polar_gap, equator_height)
    height_gap = jnp.where(polar_cycle, polar_gap, 1.0 - equator_height)
    sine_cycle = jnp.sqrt(height_gap * (1.0 + cycle_height))
    pixels = jnp.where(polar_cycle, 4.0 * cycle_number, 4.0 * nside_float)
    weight = jnp.sqrt(jnp.pi * pixels / (3.0 * nside_float * nside_float))
    return (cycle_height, sine_cycle, weight)


def legendre_seed(orders, sine_cycle):
    counter = jnp.arange(1, LMAX + 1, dtype=jnp.float32)
    log_terms = jnp.log1p(-0.5 / counter)
    partial_sum = jnp.sum(
        jnp.where(counter[None, :] <= orders[:, None], log_terms[None, :], 0.0), axis=1
    )
    head = 0.5 * jnp.log((2.0 * orders + 1.0) / (4.0 * jnp.pi)) + 0.5 * partial_sum
    return head[:, None] + orders[:, None] * jnp.log(sine_cycle)[None, :]


def recurrence_tables(orders):
    degree = jnp.arange(1, TABLE + 1, dtype=jnp.float32)[None, :]
    order_col = orders[:, None]
    alpha = jnp.sqrt(
        jnp.maximum(4.0 * degree * degree - 1.0, 1.0)
        / jnp.maximum(degree * degree - order_col * order_col, 1.0)
    )
    below = degree - 1.0
    beta = jnp.sqrt(
        jnp.maximum(below * below - order_col * order_col, 0.0)
        / jnp.maximum(4.0 * below * below - 1.0, 1.0)
    )
    return alpha.reshape(-1), (alpha * beta).reshape(-1)


def per_device(coeffs, bessel, azimuthal_order_slots):
    tracer = lax.axis_index("tracer")
    owner = lax.axis_index("dev")
    place = PLANE * tracer + lax.rem(owner, PLANE)
    plane_groups = [
        [OWNERS * t + PLANE * z + i for t in range(2) for i in range(PLANE)] for z in range(PLANES)
    ]

    away = lax.dynamic_slice_in_dim(bessel[0], (1 - tracer) * 6, 6, 0)
    partner = lax.ppermute(away, "tracer", [(0, 1), (1, 0)])

    slots_pair = jnp.repeat(azimuthal_order_slots, 2)[None, :]
    folded = fold_coefficients(slots_pair, coeffs[0])
    regrouped = lax.all_to_all(
        folded,
        ("tracer", "dev"),
        split_axis=0,
        concat_axis=0,
        tiled=True,
        axis_index_groups=plane_groups,
    )

    start = order_index(jnp.arange(CHAINS, dtype=jnp.int32), place)
    orders = (STRIDE * start).astype(jnp.float32)
    cosine, sine, weight = cycle_geometry()
    seed_log = legendre_seed(orders, sine)
    level = jnp.minimum(jnp.floor(seed_log / (STEP_LN_HIGH + STEP_LN_LOW) + 0.5), 0.0)
    seed = jnp.exp((seed_log - level * STEP_LN_HIGH) - level * STEP_LN_LOW)
    a_tab, ab_tab = recurrence_tables(orders)
    table = legendre_tables(
        start,
        a_tab,
        ab_tab,
        cosine.reshape(8, 128),
        weight.reshape(8, 128),
        seed.reshape(CHAINS, 8, 128),
        level.reshape(CHAINS, 8, 128),
    )

    harmonic = transform(table, regrouped.reshape(512, 2 * HALF))
    by_degree = lax.all_to_all(
        harmonic.reshape(256, 24, 128), ("tracer", "dev"), split_axis=0, concat_axis=0, tiled=True
    )
    who = jnp.stack([tracer, owner]).astype(jnp.int32)
    return cross_spectrum(who, by_degree.reshape(256 * 24, 128), bessel, partner)


def solution(mesh):
    placed = (P("tracer", "dev", None, None), P("tracer", "dev", None, None), P())
    return jax.shard_map(
        per_device,
        mesh=mesh,
        in_specs=placed,
        out_specs=P("tracer", "dev", None, None),
        check_vma=False,
    )
```

```python
import jax
import jax.numpy as jnp
from jax import lax
from jax.experimental import pallas as pl
from jax.experimental.pallas import tpu as pltpu
from jax.sharding import PartitionSpec as P

NSIDE = 512
CYCLES = 2047
LMAX = 1536
STRIDE = 12
HALF = 1024
PLANE = 16
PLANES = 8
OWNERS = 128
TABLE = LMAX + 16
CHAINS = 4
DEGREES_STEP = 2
CHUNK = 384
SPREAD = OWNERS // CHAINS
BLOCK_ROWS = 6 * SPREAD
STEP_LOG2 = 64.0
STEP_LN_HIGH = 44.359375
STEP_LN_LOW = 0.0020445558364884
BIG = 2.0**32
SHRINK = 2.0**-64


def half_rows(j):
    return BLOCK_ROWS * (CHAINS - j)


def table_base(j):
    return sum(2 * half_rows(i) for i in range(j))


TABLE_ROWS = table_base(CHAINS)


def order_index(j, place):
    flip = lax.rem(j, 2)
    return SPREAD * j + jnp.where(flip == 0, place, SPREAD - 1 - place)


def fold_kernel(coef_ref, out_ref):
    x = coef_ref[0]
    north = x[:, :HALF].astype(jnp.float32)
    south = x[:, HALF:]
    edge = south[:, HALF - 128 :].astype(jnp.float32)
    lane = lax.broadcasted_iota(jnp.int32, edge.shape, 1)
    edge = jnp.where(lane < 127, edge, 0.0).astype(jnp.bfloat16)
    south = jnp.concatenate([south[:, : HALF - 128], edge], axis=1)
    back_row = lax.broadcasted_iota(jnp.int32, (256, 128), 0)
    back_col = lax.broadcasted_iota(jnp.int32, (256, 128), 1)
    back = jnp.where(back_row + back_col == 254, 1.0, 0.0).astype(jnp.bfloat16)
    for b in range(8):
        if b < 7:
            mirrored = jnp.dot(
                south[:, 128 * (6 - b) : 128 * (8 - b)], back, preferred_element_type=jnp.float32
            )
        else:
            mirrored = jnp.dot(south[:, :128], back[128:], preferred_element_type=jnp.float32)
        here = north[:, 128 * b : 128 * (b + 1)]
        even = (here + mirrored).astype(jnp.bfloat16)
        odd = (here - mirrored).astype(jnp.bfloat16)
        out_ref[:, 0, :, 128 * b : 128 * (b + 1)] = even.reshape(32, 8, 128)
        out_ref[:, 0, :, HALF + 128 * b : HALF + 128 * (b + 1)] = odd.reshape(32, 8, 128)


def fold_coefficients(slots, coeffs):
    row = jnp.arange(256, dtype=jnp.int32)
    j = (row % 8) // 2
    place = jnp.where(j % 2 == 0, row // 8, SPREAD - 1 - row // 8)
    wanted = STRIDE * (SPREAD * j + place)
    hit = jnp.logical_and(
        jnp.repeat(slots, 2)[None, :] == wanted[:, None], row[None, :] % 2 == row[:, None] % 2
    )
    picked = jnp.einsum(
        "pr,src->spc", hit.astype(jnp.bfloat16), coeffs, preferred_element_type=jnp.float32
    ).astype(jnp.bfloat16)
    return pl.pallas_call(
        fold_kernel,
        grid=(2,),
        in_specs=[pl.BlockSpec((1, 256, 2 * HALF), lambda s: (s, 0, 0))],
        out_specs=pl.BlockSpec((32, 1, 8, 2 * HALF), lambda s: (0, s, 0, 0)),
        out_shape=pltpu.HBM((32, 2, 8, 2 * HALF), jnp.bfloat16),
        compiler_params=pltpu.CompilerParams(vmem_limit_bytes=16 * 2**20),
        name="fold",
    )(picked)


def legendre_kernel(
    start_ref, a_ref, ab_ref, cos_ref, weight_ref, seed_ref, level_ref, out_ref, rows_ref
):
    x = cos_ref[...]
    weight = weight_ref[...]
    zero = jnp.zeros((8, 128), jnp.float32)

    for j in range(CHAINS):
        for h in range(2):
            first = table_base(j) + h * half_rows(j)

            def clear(r, carry, first=first):
                rows_ref[pl.ds(pl.multiple_of(8 * (first + r), 8), 8), :] = zero
                return carry

            lax.fori_loop(0, BLOCK_ROWS, clear, 0, unroll=8)

    tracks = CHAINS // 2

    def advance(it, state):
        new_state = []
        for t in range(tracks):
            ja, jb = t, CHAINS - 1 - t
            prev, cur, level = state[t]
            ka, kb = start_ref[ja], start_ref[jb]
            first_len = OWNERS - ka
            in_a = it < first_len
            d = jnp.where(in_a, ka + it, kb + it - first_len)
            k = jnp.where(in_a, ka, kb)
            j = jnp.where(in_a, ja, jb)
            fresh = d == k
            prev = jnp.where(fresh, 0.0, prev)
            cur = jnp.where(fresh, seed_ref[j], cur)
            level = jnp.where(fresh, level_ref[j], level)
            biggest = jnp.maximum(jnp.abs(prev), jnp.abs(cur))
            over = biggest > BIG
            factor = jnp.where(over, SHRINK, 1.0)
            prev = prev * factor
            cur = cur * factor
            level = level + jnp.where(over, 1.0, 0.0)
            scale = weight * jnp.exp2(level * STEP_LOG2)
            coef = j * TABLE + STRIDE * d
            per_half = jnp.where(in_a, half_rows(ja), half_rows(jb))
            first = jnp.where(in_a, table_base(ja), table_base(jb)) + 6 * (d - SPREAD * j)
            for i in range(STRIDE):
                h, within = divmod(i, 6)
                spot = 8 * (first + h * per_half + within)
                rows_ref[pl.ds(pl.multiple_of(spot, 8), 8), :] = cur * scale
                nxt = (a_ref[coef + i] * x) * cur - ab_ref[coef + i] * prev
                prev, cur = cur, nxt
            new_state.append((prev, cur, level))
        return tuple(new_state)

    lax.fori_loop(0, OWNERS + 1, advance, ((zero, zero, zero),) * tracks)

    def pack(block, carry):
        r0 = pl.multiple_of(block * 16, 16)
        for s in range(8):
            v = rows_ref[pl.ds(8 * r0 + s, 16, stride=8), :]
            out_ref[s, pl.ds(r0, 16), :] = v.astype(jnp.bfloat16)
        return carry

    lax.fori_loop(0, TABLE_ROWS // 16, pack, 0, unroll=2)


def legendre_tables(start, a_tab, ab_tab, cosine, weight, seed, level):
    smem = pl.BlockSpec(memory_space=pltpu.SMEM)
    vmem = pl.BlockSpec(memory_space=pltpu.VMEM)
    return pl.pallas_call(
        legendre_kernel,
        in_specs=[smem, smem, smem, vmem, vmem, vmem, vmem],
        out_specs=vmem,
        out_shape=jax.ShapeDtypeStruct((8, TABLE_ROWS, 128), jnp.bfloat16),
        scratch_shapes=[pltpu.VMEM((8 * TABLE_ROWS, 128), jnp.float32)],
        compiler_params=pltpu.CompilerParams(vmem_limit_bytes=28 * 2**20),
        name="legendre",
    )(start, a_tab, ab_tab, cosine, weight, seed, level)


def transform_kernel(table_hbm, x_ref, out_hbm, table, picked, wide, packed, sems):
    copies = []
    for h in range(2):
        for j in range(CHAINS):
            span = pl.ds(table_base(j) + h * half_rows(j), half_rows(j))
            copy = pltpu.make_async_copy(
                table_hbm.at[:, span], table.at[:, span], sems.at[CHAINS * h + j]
            )
            copy.start()
            copies.append(copy)
    row = lax.broadcasted_iota(jnp.int32, (256, 256), 0)
    col = lax.broadcasted_iota(jnp.int32, (256, 256), 1)
    shell = row % 32
    source = (shell // 2) * 16 + (shell % 2) * 8 + (row // 64) * 2 + (row % 64) // 32
    pick = jnp.where(source == col, 1.0, 0.0).astype(jnp.bfloat16)
    for t in range(2):
        got = jnp.dot(
            pick, x_ref[256 * t : 256 * (t + 1), :], preferred_element_type=jnp.float32
        ).astype(jnp.bfloat16)
        for j in range(CHAINS):
            mine = got[64 * j : 64 * (j + 1)]
            picked[j, 64 * t : 64 * (t + 1), :] = mine[:, :HALF]
            picked[j, 128 + 64 * t : 128 + 64 * (t + 1), :] = mine[:, HALF:]
    contract = (((1,), (1,)), ((), ()))
    for h in range(2):
        for j in range(CHAINS):
            copies[CHAINS * h + j].wait()
            gap = BLOCK_ROWS * j
            base = h * 4 * half_rows(0) + j
            if gap:
                wide[pl.ds(base, gap, stride=4), :] = jnp.zeros((gap, 128), jnp.float32)
            for done in range(0, half_rows(j), CHUNK):
                size = min(CHUNK, half_rows(j) - done)
                first = table_base(j) + h * half_rows(j) + done
                rows = jnp.concatenate(
                    [table[s, first : first + size, :] for s in range(8)], axis=1
                )
                got = lax.dot_general(rows, picked[j], contract, preferred_element_type=jnp.float32)
                parity = lax.broadcasted_iota(jnp.int32, (size, 128), 0) % 2
                wide[pl.ds(base + 4 * (gap + done), size, stride=4), :] = jnp.where(
                    parity == 0, got[:, :128], got[:, 128:]
                )
        half = pl.ds(h * 4 * half_rows(0), 4 * half_rows(0))
        packed[half, :] = wide[half, :].astype(jnp.bfloat16)
        copy = pltpu.make_async_copy(packed.at[half], out_hbm.at[half], sems.at[2 * CHAINS + h])
        copy.start()
        copies.append(copy)
    for copy in copies[2 * CHAINS :]:
        copy.wait()


def transform(table, x):
    rows = 8 * half_rows(0)
    vmem = pl.BlockSpec(memory_space=pltpu.VMEM)
    return pl.pallas_call(
        transform_kernel,
        in_specs=[pl.BlockSpec(memory_space=pl.ANY), vmem],
        out_specs=pl.BlockSpec(memory_space=pltpu.HBM),
        out_shape=pltpu.HBM((rows, 128), jnp.bfloat16),
        scratch_shapes=[
            pltpu.VMEM((8, TABLE_ROWS, 128), jnp.bfloat16),
            pltpu.VMEM((CHAINS, 256, HALF), jnp.bfloat16),
            pltpu.VMEM((rows, 128), jnp.float32),
            pltpu.VMEM((rows, 128), jnp.bfloat16),
            pltpu.SemaphoreType.DMA((2 * CHAINS + 2,)),
        ],
        compiler_params=pltpu.CompilerParams(vmem_limit_bytes=24 * 2**20),
        name="transform",
    )(pltpu.with_memory_space_constraint(table, pltpu.HBM), x)


def degree_fields(wide, i):
    lane = lax.broadcasted_iota(jnp.int32, (PLANE, 128), 1) // 32
    blocks = [[], []]
    for core in range(2):
        for j in range(CHAINS):
            tiles = [[], [], [], []]
            for zh in range(2):
                turned = []
                for z4 in range(4):
                    source = (core * OWNERS + (4 * zh + z4) * PLANE) * 24
                    v = wide[pl.ds(source + 4 * i + j, PLANE, stride=24), :]
                    turned.append(
                        [v] + [pltpu.roll(v, shift=32 * turn, axis=1) for turn in (1, 2, 3)]
                    )
                for part in range(4):
                    tile = turned[0][(0 - part) % 4]
                    for z4 in range(1, 4):
                        tile = jnp.where(lane == z4, turned[z4][(z4 - part) % 4], tile)
                    tiles[part].append(tile)
            for part in range(4):
                blocks[part // 2].append(
                    jnp.concatenate(tiles[part], axis=1).astype(jnp.bfloat16)
                )
    return [jnp.concatenate(rows, axis=0) for rows in blocks]


def cross_kernel(who_ref, harm_ref, own_ref, other_ref, out_ref, wide):
    step = pl.program_id(0)

    @pl.when(step == 0)
    def _():
        wide[...] = harm_ref[...].astype(jnp.float32)

    tracer, owner = who_ref[0], who_ref[1]
    first = tracer == 0
    tally = jnp.full((1, 512), owner + 1, jnp.int32).astype(jnp.float32)
    factor = 1.0 / jnp.sqrt(2.0 * tally)
    contract = (((1,), (1,)), ((), ()))
    for e in range(DEGREES_STEP):
        fields = degree_fields(wide, DEGREES_STEP * step + e)
        own, other = own_ref[0, e], other_ref[e]
        basis_lead = jnp.where(first, own, other)
        basis_trail = jnp.where(first, other, own)
        lead = lax.dot_general(basis_lead, fields[0], contract, preferred_element_type=jnp.float32)
        trail = lax.dot_general(
            fields[1], basis_trail, contract, preferred_element_type=jnp.float32
        )
        total = jnp.dot(
            lead.astype(jnp.bfloat16),
            trail.astype(jnp.bfloat16),
            preferred_element_type=jnp.float32,
        )
        out_ref[0, e] = total * factor


def cross_spectrum(who, harmonic, bessel, partner):
    steps = 6 // DEGREES_STEP
    return pl.pallas_call(
        cross_kernel,
        grid_spec=pltpu.PrefetchScalarGridSpec(
            num_scalar_prefetch=1,
            grid=(steps,),
            in_specs=[
                pl.BlockSpec((256 * 24, 128), lambda i, who: (0, 0)),
                pl.BlockSpec(
                    (1, DEGREES_STEP, 512, 256), lambda i, who: (0, steps * who[0] + i, 0, 0)
                ),
                pl.BlockSpec((DEGREES_STEP, 512, 256), lambda i, who: (i, 0, 0)),
            ],
            out_specs=pl.BlockSpec((1, DEGREES_STEP, 512, 512), lambda i, who: (0, i, 0, 0)),
            scratch_shapes=[pltpu.VMEM((256 * 24, 128), jnp.float32)],
        ),
        out_shape=jax.ShapeDtypeStruct((1, 6, 512, 512), jnp.float32),
        compiler_params=pltpu.CompilerParams(vmem_limit_bytes=24 * 2**20),
        name="cross",
    )(
        who,
        harmonic,
        pltpu.with_memory_space_constraint(bessel, pltpu.HBM),
        pltpu.with_memory_space_constraint(partner, pltpu.HBM),
    )


def cycle_geometry():
    cycle_number = jnp.arange(1, HALF + 1, dtype=jnp.float32)
    nside_float = jnp.float32(NSIDE)
    polar_cycle = cycle_number < nside_float
    polar_gap = cycle_number * cycle_number / (3.0 * nside_float * nside_float)
    equator_height = 4.0 / 3.0 - 2.0 * cycle_number / (3.0 * nside_float)
    cycle_height = jnp.where(polar_cycle, 1.0 - polar_gap, equator_height)
    height_gap = jnp.where(polar_cycle, polar_gap, 1.0 - equator_height)
    sine_cycle = jnp.sqrt(height_gap * (1.0 + cycle_height))
    pixels = jnp.where(polar_cycle, 4.0 * cycle_number, 4.0 * nside_float)
    weight = jnp.sqrt(jnp.pi * pixels / (3.0 * nside_float * nside_float))
    return (cycle_height, sine_cycle, weight)


def legendre_seed(orders, sine_cycle):
    counter = jnp.arange(1, LMAX + 1, dtype=jnp.float32)
    log_terms = jnp.log1p(-0.5 / counter)
    partial_sum = jnp.sum(
        jnp.where(counter[None, :] <= orders[:, None], log_terms[None, :], 0.0), axis=1
    )
    head = 0.5 * jnp.log((2.0 * orders + 1.0) / (4.0 * jnp.pi)) + 0.5 * partial_sum
    return head[:, None] + orders[:, None] * jnp.log(sine_cycle)[None, :]


def recurrence_tables(orders):
    degree = jnp.arange(1, TABLE + 1, dtype=jnp.float32)[None, :]
    order_col = orders[:, None]
    alpha = jnp.sqrt(
        jnp.maximum(4.0 * degree * degree - 1.0, 1.0)
        / jnp.maximum(degree * degree - order_col * order_col, 1.0)
    )
    below = degree - 1.0
    beta = jnp.sqrt(
        jnp.maximum(below * below - order_col * order_col, 0.0)
        / jnp.maximum(4.0 * below * below - 1.0, 1.0)
    )
    return alpha.reshape(-1), (alpha * beta).reshape(-1)


def per_device(coeffs, bessel, azimuthal_order_slots):
    tracer = lax.axis_index("tracer")
    owner = lax.axis_index("dev")
    place = PLANE * tracer + lax.rem(owner, PLANE)
    plane_groups = [
        [OWNERS * t + PLANE * z + i for t in range(2) for i in range(PLANE)] for z in range(PLANES)
    ]

    away = lax.dynamic_slice_in_dim(bessel[0], (1 - tracer) * 6, 6, 0)
    partner = lax.ppermute(away, "tracer", [(0, 1), (1, 0)])

    folded = fold_coefficients(azimuthal_order_slots, coeffs[0])
    regrouped = lax.all_to_all(
        folded,
        ("tracer", "dev"),
        split_axis=0,
        concat_axis=0,
        tiled=True,
        axis_index_groups=plane_groups,
    )

    start = order_index(jnp.arange(CHAINS, dtype=jnp.int32), place)
    orders = (STRIDE * start).astype(jnp.float32)
    cosine, sine, weight = cycle_geometry()
    seed_log = legendre_seed(orders, sine)
    level = jnp.minimum(jnp.floor(seed_log / (STEP_LN_HIGH + STEP_LN_LOW) + 0.5), 0.0)
    seed = jnp.exp((seed_log - level * STEP_LN_HIGH) - level * STEP_LN_LOW)
    a_tab, ab_tab = recurrence_tables(orders)
    table = legendre_tables(
        start,
        a_tab,
        ab_tab,
        cosine.reshape(8, 128),
        weight.reshape(8, 128),
        seed.reshape(CHAINS, 8, 128),
        level.reshape(CHAINS, 8, 128),
    )

    harmonic = transform(table, regrouped.reshape(512, 2 * HALF))
    by_degree = lax.all_to_all(
        harmonic.reshape(256, 24, 128), ("tracer", "dev"), split_axis=0, concat_axis=0, tiled=True
    )
    who = jnp.stack([tracer, owner]).astype(jnp.int32)
    return cross_spectrum(who, by_degree.reshape(256 * 24, 128), bessel, partner)


def solution(mesh):
    placed = (P("tracer", "dev", None, None), P("tracer", "dev", None, None), P())
    return jax.shard_map(
        per_device,
        mesh=mesh,
        in_specs=placed,
        out_specs=P("tracer", "dev", None, None),
        check_vma=False,
    )
```

```python
import jax
import jax.numpy as jnp
from jax import lax
from jax.experimental import pallas as pl
from jax.experimental.pallas import tpu as pltpu
from jax.sharding import PartitionSpec as P

NSIDE = 512
CYCLES = 2047
LMAX = 1536
STRIDE = 12
HALF = 1024
PLANE = 16
PLANES = 8
OWNERS = 128
TABLE = LMAX + 16
CHAINS = 4
DEGREES = 6
CHUNK = 384
SPREAD = OWNERS // CHAINS
BLOCK_ROWS = 6 * SPREAD
STEP_LOG2 = 64.0
STEP_LN_HIGH = 44.359375
STEP_LN_LOW = 0.0020445558364884
BIG = 2.0**32
SHRINK = 2.0**-64


def half_rows(j):
    return BLOCK_ROWS * (CHAINS - j)


def table_base(j):
    return sum(2 * half_rows(i) for i in range(j))


TABLE_ROWS = table_base(CHAINS)


def order_index(j, place):
    flip = lax.rem(j, 2)
    return SPREAD * j + jnp.where(flip == 0, place, SPREAD - 1 - place)


def fold_kernel(coef_ref, out_ref):
    x = coef_ref[0]
    north = x[:, :HALF].astype(jnp.float32)
    south = x[:, HALF:]
    edge = south[:, HALF - 128 :].astype(jnp.float32)
    lane = lax.broadcasted_iota(jnp.int32, edge.shape, 1)
    edge = jnp.where(lane < 127, edge, 0.0).astype(jnp.bfloat16)
    south = jnp.concatenate([south[:, : HALF - 128], edge], axis=1)
    back_row = lax.broadcasted_iota(jnp.int32, (256, 128), 0)
    back_col = lax.broadcasted_iota(jnp.int32, (256, 128), 1)
    back = jnp.where(back_row + back_col == 254, 1.0, 0.0).astype(jnp.bfloat16)
    for b in range(8):
        if b < 7:
            mirrored = jnp.dot(
                south[:, 128 * (6 - b) : 128 * (8 - b)], back, preferred_element_type=jnp.float32
            )
        else:
            mirrored = jnp.dot(south[:, :128], back[128:], preferred_element_type=jnp.float32)
        here = north[:, 128 * b : 128 * (b + 1)]
        even = (here + mirrored).astype(jnp.bfloat16)
        odd = (here - mirrored).astype(jnp.bfloat16)
        out_ref[:, 0, :, 128 * b : 128 * (b + 1)] = even.reshape(32, 8, 128)
        out_ref[:, 0, :, HALF + 128 * b : HALF + 128 * (b + 1)] = odd.reshape(32, 8, 128)


def fold_coefficients(slots, coeffs):
    row = jnp.arange(256, dtype=jnp.int32)
    j = (row % 8) // 2
    place = jnp.where(j % 2 == 0, row // 8, SPREAD - 1 - row // 8)
    wanted = STRIDE * (SPREAD * j + place)
    hit = jnp.logical_and(
        jnp.repeat(slots, 2)[None, :] == wanted[:, None], row[None, :] % 2 == row[:, None] % 2
    )
    picked = jnp.einsum(
        "pr,src->spc", hit.astype(jnp.bfloat16), coeffs, preferred_element_type=jnp.float32
    ).astype(jnp.bfloat16)
    return pl.pallas_call(
        fold_kernel,
        grid=(2,),
        in_specs=[pl.BlockSpec((1, 256, 2 * HALF), lambda s: (s, 0, 0))],
        out_specs=pl.BlockSpec((32, 1, 8, 2 * HALF), lambda s: (0, s, 0, 0)),
        out_shape=pltpu.HBM((32, 2, 8, 2 * HALF), jnp.bfloat16),
        compiler_params=pltpu.CompilerParams(vmem_limit_bytes=16 * 2**20),
        name="fold",
    )(picked)


def legendre_kernel(
    start_ref, a_ref, ab_ref, cos_ref, weight_ref, seed_ref, level_ref, out_ref, rows_ref
):
    x = cos_ref[...]
    weight = weight_ref[...]
    zero = jnp.zeros((8, 128), jnp.float32)

    for j in range(CHAINS):
        for h in range(2):
            first = table_base(j) + h * half_rows(j)

            def clear(r, carry, first=first):
                rows_ref[pl.ds(pl.multiple_of(8 * (first + r), 8), 8), :] = zero
                return carry

            lax.fori_loop(0, BLOCK_ROWS, clear, 0, unroll=8)

    tracks = CHAINS // 2

    def advance(it, state):
        new_state = []
        for t in range(tracks):
            ja, jb = t, CHAINS - 1 - t
            prev, cur, level = state[t]
            ka, kb = start_ref[ja], start_ref[jb]
            first_len = OWNERS - ka
            in_a = it < first_len
            d = jnp.where(in_a, ka + it, kb + it - first_len)
            k = jnp.where(in_a, ka, kb)
            j = jnp.where(in_a, ja, jb)
            fresh = d == k
            prev = jnp.where(fresh, 0.0, prev)
            cur = jnp.where(fresh, seed_ref[j], cur)
            level = jnp.where(fresh, level_ref[j], level)
            biggest = jnp.maximum(jnp.abs(prev), jnp.abs(cur))
            over = biggest > BIG
            factor = jnp.where(over, SHRINK, 1.0)
            prev = prev * factor
            cur = cur * factor
            level = level + jnp.where(over, 1.0, 0.0)
            scale = weight * jnp.exp2(level * STEP_LOG2)
            coef = j * TABLE + STRIDE * d
            per_half = jnp.where(in_a, half_rows(ja), half_rows(jb))
            first = jnp.where(in_a, table_base(ja), table_base(jb)) + 6 * (d - SPREAD * j)
            for i in range(STRIDE):
                h, within = divmod(i, 6)
                spot = 8 * (first + h * per_half + within)
                rows_ref[pl.ds(pl.multiple_of(spot, 8), 8), :] = cur * scale
                nxt = (a_ref[coef + i] * x) * cur - ab_ref[coef + i] * prev
                prev, cur = cur, nxt
            new_state.append((prev, cur, level))
        return tuple(new_state)

    lax.fori_loop(0, OWNERS + 1, advance, ((zero, zero, zero),) * tracks)

    def pack(block, carry):
        r0 = pl.multiple_of(block * 16, 16)
        for s in range(8):
            v = rows_ref[pl.ds(8 * r0 + s, 16, stride=8), :]
            out_ref[s, pl.ds(r0, 16), :] = v.astype(jnp.bfloat16)
        return carry

    lax.fori_loop(0, TABLE_ROWS // 16, pack, 0, unroll=2)


def legendre_tables(start, a_tab, ab_tab, cosine, weight, seed, level):
    smem = pl.BlockSpec(memory_space=pltpu.SMEM)
    vmem = pl.BlockSpec(memory_space=pltpu.VMEM)
    return pl.pallas_call(
        legendre_kernel,
        in_specs=[smem, smem, smem, vmem, vmem, vmem, vmem],
        out_specs=vmem,
        out_shape=jax.ShapeDtypeStruct((8, TABLE_ROWS, 128), jnp.bfloat16),
        scratch_shapes=[pltpu.VMEM((8 * TABLE_ROWS, 128), jnp.float32)],
        compiler_params=pltpu.CompilerParams(vmem_limit_bytes=28 * 2**20),
        name="legendre",
    )(start, a_tab, ab_tab, cosine, weight, seed, level)


def transform_kernel(table_hbm, x_hbm, out_hbm, table, x_ref, picked, wide, packed, sems):
    loads = []
    for t in range(2):
        span = pl.ds(256 * t, 256)
        copy = pltpu.make_async_copy(
            x_hbm.at[span], x_ref.at[span], sems.at[2 * CHAINS + 2 + t]
        )
        copy.start()
        loads.append(copy)
    copies = []
    for h in range(2):
        for j in range(CHAINS):
            span = pl.ds(table_base(j) + h * half_rows(j), half_rows(j))
            copy = pltpu.make_async_copy(
                table_hbm.at[:, span], table.at[:, span], sems.at[CHAINS * h + j]
            )
            copy.start()
            copies.append(copy)
    row = lax.broadcasted_iota(jnp.int32, (256, 256), 0)
    col = lax.broadcasted_iota(jnp.int32, (256, 256), 1)
    shell = row % 32
    source = (shell // 2) * 16 + (shell % 2) * 8 + (row // 64) * 2 + (row % 64) // 32
    pick = jnp.where(source == col, 1.0, 0.0).astype(jnp.bfloat16)
    for copy in loads:
        copy.wait()
    for t in range(2):
        got = jnp.dot(
            pick, x_ref[256 * t : 256 * (t + 1), :], preferred_element_type=jnp.float32
        ).astype(jnp.bfloat16)
        for j in range(CHAINS):
            mine = got[64 * j : 64 * (j + 1)]
            picked[j, 64 * t : 64 * (t + 1), :] = mine[:, :HALF]
            picked[j, 128 + 64 * t : 128 + 64 * (t + 1), :] = mine[:, HALF:]
    contract = (((1,), (1,)), ((), ()))
    for h in range(2):
        for j in range(CHAINS):
            copies[CHAINS * h + j].wait()
        for j in range(CHAINS):
            gap = BLOCK_ROWS * j
            base = h * 4 * half_rows(0) + j
            if gap:
                wide[pl.ds(base, gap, stride=4), :] = jnp.zeros((gap, 128), jnp.float32)
            for done in range(0, half_rows(j), CHUNK):
                size = min(CHUNK, half_rows(j) - done)
                first = table_base(j) + h * half_rows(j) + done
                rows = jnp.concatenate(
                    [table[s, first : first + size, :] for s in range(8)], axis=1
                )
                got = lax.dot_general(rows, picked[j], contract, preferred_element_type=jnp.float32)
                parity = lax.broadcasted_iota(jnp.int32, (size, 128), 0) % 2
                wide[pl.ds(base + 4 * (gap + done), size, stride=4), :] = jnp.where(
                    parity == 0, got[:, :128], got[:, 128:]
                )
        half = pl.ds(h * 4 * half_rows(0), 4 * half_rows(0))
        packed[half, :] = wide[half, :].astype(jnp.bfloat16)
        copy = pltpu.make_async_copy(packed.at[half], out_hbm.at[half], sems.at[2 * CHAINS + h])
        copy.start()
        copies.append(copy)
    for copy in copies[2 * CHAINS :]:
        copy.wait()


def transform(table, x):
    rows = 8 * half_rows(0)
    hbm = pl.BlockSpec(memory_space=pl.ANY)
    return pl.pallas_call(
        transform_kernel,
        in_specs=[hbm, hbm],
        out_specs=pl.BlockSpec(memory_space=pltpu.HBM),
        out_shape=pltpu.HBM((rows, 128), jnp.bfloat16),
        scratch_shapes=[
            pltpu.VMEM((8, TABLE_ROWS, 128), jnp.bfloat16),
            pltpu.VMEM((512, 2 * HALF), jnp.bfloat16),
            pltpu.VMEM((CHAINS, 256, HALF), jnp.bfloat16),
            pltpu.VMEM((rows, 128), jnp.float32),
            pltpu.VMEM((rows, 128), jnp.bfloat16),
            pltpu.SemaphoreType.DMA((2 * CHAINS + 4,)),
        ],
        compiler_params=pltpu.CompilerParams(vmem_limit_bytes=24 * 2**20),
        name="transform",
    )(
        pltpu.with_memory_space_constraint(table, pltpu.HBM),
        pltpu.with_memory_space_constraint(x, pltpu.HBM),
    )


def degree_fields(wide, i):
    lane = lax.broadcasted_iota(jnp.int32, (PLANE, 128), 1) // 32
    blocks = [[], []]
    for core in range(2):
        for j in range(CHAINS):
            tiles = [[], [], [], []]
            for zh in range(2):
                turned = []
                for z4 in range(4):
                    source = (core * OWNERS + (4 * zh + z4) * PLANE) * 24
                    v = wide[pl.ds(source + 4 * i + j, PLANE, stride=24), :]
                    turned.append(
                        [v] + [pltpu.roll(v, shift=32 * turn, axis=1) for turn in (1, 2, 3)]
                    )
                for part in range(4):
                    tile = turned[0][(0 - part) % 4]
                    for z4 in range(1, 4):
                        tile = jnp.where(lane == z4, turned[z4][(z4 - part) % 4], tile)
                    tiles[part].append(tile)
            for part in range(4):
                blocks[part // 2].append(
                    jnp.concatenate(tiles[part], axis=1).astype(jnp.bfloat16)
                )
    return [jnp.concatenate(rows, axis=0) for rows in blocks]


def cross_kernel(
    who_ref, harm_hbm, own_hbm, other_hbm, out_hbm, harm, wide, own, other, out, sems
):
    tracer, owner = who_ref[0], who_ref[1]
    part = OWNERS * 24
    arrivals = []
    for core in range(2):
        span = pl.ds(core * part, part)
        arrivals.append(pltpu.make_async_copy(harm_hbm.at[span], harm.at[span], sems.at[core]))
    for e in range(DEGREES):
        arrivals.append(
            pltpu.make_async_copy(own_hbm.at[0, DEGREES * tracer + e], own.at[e], sems.at[2 + e])
        )
        arrivals.append(
            pltpu.make_async_copy(other_hbm.at[e], other.at[e], sems.at[2 + DEGREES + e])
        )
    for copy in arrivals:
        copy.start()
    for core in range(2):
        arrivals[core].wait()
        span = pl.ds(core * part, part)
        wide[span, :] = harm[span, :].astype(jnp.float32)
    first = tracer == 0
    tally = jnp.full((1, 512), owner + 1, jnp.int32).astype(jnp.float32)
    factor = 1.0 / jnp.sqrt(2.0 * tally)
    contract = (((1,), (1,)), ((), ()))
    departures = []
    for e0 in range(0, DEGREES, 3):
        group = range(e0, e0 + 3)
        for e in group:
            arrivals[2 + 2 * e].wait()
            arrivals[3 + 2 * e].wait()
        for e in group:
            fields = degree_fields(wide, e)
            mine, theirs = own[e], other[e]
            basis_lead = jnp.where(first, mine, theirs)
            basis_trail = jnp.where(first, theirs, mine)
            lead = lax.dot_general(
                basis_lead, fields[0], contract, preferred_element_type=jnp.float32
            )
            trail = lax.dot_general(
                fields[1], basis_trail, contract, preferred_element_type=jnp.float32
            )
            total = jnp.dot(
                lead.astype(jnp.bfloat16),
                trail.astype(jnp.bfloat16),
                preferred_element_type=jnp.float32,
            )
            out[e] = total * factor
        for e in group:
            copy = pltpu.make_async_copy(
                out.at[e], out_hbm.at[0, e], sems.at[2 + 2 * DEGREES + e]
            )
            copy.start()
            departures.append(copy)
    for copy in departures:
        copy.wait()


def cross_spectrum(who, harmonic, bessel, partner):
    hbm = pl.BlockSpec(memory_space=pl.ANY)
    rows = 2 * OWNERS * 24
    return pl.pallas_call(
        cross_kernel,
        in_specs=[pl.BlockSpec(memory_space=pltpu.SMEM), hbm, hbm, hbm],
        out_specs=hbm,
        out_shape=jax.ShapeDtypeStruct((1, DEGREES, 512, 512), jnp.float32),
        scratch_shapes=[
            pltpu.VMEM((rows, 128), jnp.bfloat16),
            pltpu.VMEM((rows, 128), jnp.float32),
            pltpu.VMEM((DEGREES, 512, 256), jnp.bfloat16),
            pltpu.VMEM((DEGREES, 512, 256), jnp.bfloat16),
            pltpu.VMEM((DEGREES, 512, 512), jnp.float32),
            pltpu.SemaphoreType.DMA((2 + 3 * DEGREES,)),
        ],
        compiler_params=pltpu.CompilerParams(vmem_limit_bytes=32 * 2**20),
        name="cross",
    )(
        who,
        pltpu.with_memory_space_constraint(harmonic, pltpu.HBM),
        pltpu.with_memory_space_constraint(bessel, pltpu.HBM),
        pltpu.with_memory_space_constraint(partner, pltpu.HBM),
    )


def cycle_geometry():
    cycle_number = jnp.arange(1, HALF + 1, dtype=jnp.float32)
    nside_float = jnp.float32(NSIDE)
    polar_cycle = cycle_number < nside_float
    polar_gap = cycle_number * cycle_number / (3.0 * nside_float * nside_float)
    equator_height = 4.0 / 3.0 - 2.0 * cycle_number / (3.0 * nside_float)
    cycle_height = jnp.where(polar_cycle, 1.0 - polar_gap, equator_height)
    height_gap = jnp.where(polar_cycle, polar_gap, 1.0 - equator_height)
    sine_cycle = jnp.sqrt(height_gap * (1.0 + cycle_height))
    pixels = jnp.where(polar_cycle, 4.0 * cycle_number, 4.0 * nside_float)
    weight = jnp.sqrt(jnp.pi * pixels / (3.0 * nside_float * nside_float))
    return (cycle_height, sine_cycle, weight)


def legendre_seed(orders, sine_cycle):
    counter = jnp.arange(1, LMAX + 1, dtype=jnp.float32)
    log_terms = jnp.log1p(-0.5 / counter)
    partial_sum = jnp.sum(
        jnp.where(counter[None, :] <= orders[:, None], log_terms[None, :], 0.0), axis=1
    )
    head = 0.5 * jnp.log((2.0 * orders + 1.0) / (4.0 * jnp.pi)) + 0.5 * partial_sum
    return head[:, None] + orders[:, None] * jnp.log(sine_cycle)[None, :]


def recurrence_tables(orders):
    degree = jnp.arange(1, TABLE + 1, dtype=jnp.float32)[None, :]
    order_col = orders[:, None]
    alpha = jnp.sqrt(
        jnp.maximum(4.0 * degree * degree - 1.0, 1.0)
        / jnp.maximum(degree * degree - order_col * order_col, 1.0)
    )
    below = degree - 1.0
    beta = jnp.sqrt(
        jnp.maximum(below * below - order_col * order_col, 0.0)
        / jnp.maximum(4.0 * below * below - 1.0, 1.0)
    )
    return alpha.reshape(-1), (alpha * beta).reshape(-1)


def per_device(coeffs, bessel, azimuthal_order_slots):
    tracer = lax.axis_index("tracer")
    owner = lax.axis_index("dev")
    place = PLANE * tracer + lax.rem(owner, PLANE)
    plane_groups = [
        [OWNERS * t + PLANE * z + i for t in range(2) for i in range(PLANE)] for z in range(PLANES)
    ]

    away = lax.dynamic_slice_in_dim(bessel[0], (1 - tracer) * 6, 6, 0)
    partner = lax.ppermute(away, "tracer", [(0, 1), (1, 0)])

    folded = fold_coefficients(azimuthal_order_slots, coeffs[0])
    regrouped = lax.all_to_all(
        folded,
        ("tracer", "dev"),
        split_axis=0,
        concat_axis=0,
        tiled=True,
        axis_index_groups=plane_groups,
    )

    start = order_index(jnp.arange(CHAINS, dtype=jnp.int32), place)
    orders = (STRIDE * start).astype(jnp.float32)
    cosine, sine, weight = cycle_geometry()
    seed_log = legendre_seed(orders, sine)
    level = jnp.minimum(jnp.floor(seed_log / (STEP_LN_HIGH + STEP_LN_LOW) + 0.5), 0.0)
    seed = jnp.exp((seed_log - level * STEP_LN_HIGH) - level * STEP_LN_LOW)
    a_tab, ab_tab = recurrence_tables(orders)
    table = legendre_tables(
        start,
        a_tab,
        ab_tab,
        cosine.reshape(8, 128),
        weight.reshape(8, 128),
        seed.reshape(CHAINS, 8, 128),
        level.reshape(CHAINS, 8, 128),
    )

    harmonic = transform(table, regrouped.reshape(512, 2 * HALF))
    by_degree = lax.all_to_all(
        harmonic.reshape(256, 24, 128), ("tracer", "dev"), split_axis=0, concat_axis=0, tiled=True
    )
    who = jnp.stack([tracer, owner]).astype(jnp.int32)
    return cross_spectrum(who, by_degree.reshape(256 * 24, 128), bessel, partner)


def solution(mesh):
    placed = (P("tracer", "dev", None, None), P("tracer", "dev", None, None), P())
    return jax.shard_map(
        per_device,
        mesh=mesh,
        in_specs=placed,
        out_specs=P("tracer", "dev", None, None),
        check_vma=False,
    )
```

```python
import jax
import jax.numpy as jnp
from jax import lax
from jax.experimental import pallas as pl
from jax.experimental.pallas import tpu as pltpu
from jax.sharding import PartitionSpec as P

NSIDE = 512
CYCLES = 2047
LMAX = 1536
STRIDE = 12
HALF = 1024
PLANE = 16
PLANES = 8
OWNERS = 128
TABLE = LMAX + 16
CHAINS = 4
DEGREES = 6
CHUNK = 384
SPREAD = OWNERS // CHAINS
BLOCK_ROWS = 6 * SPREAD
STEP_LOG2 = 64.0
STEP_LN_HIGH = 44.359375
STEP_LN_LOW = 0.0020445558364884
BIG = 2.0**32
SHRINK = 2.0**-64


def half_rows(j):
    return BLOCK_ROWS * (CHAINS - j)


def table_base(j):
    return sum(2 * half_rows(i) for i in range(j))


TABLE_ROWS = table_base(CHAINS)


def order_index(j, place):
    flip = lax.rem(j, 2)
    return SPREAD * j + jnp.where(flip == 0, place, SPREAD - 1 - place)


def fold_kernel(coef_ref, out_ref):
    x = coef_ref[0]
    north = x[:, :HALF].astype(jnp.float32)
    south = x[:, HALF:]
    edge = south[:, HALF - 128 :].astype(jnp.float32)
    lane = lax.broadcasted_iota(jnp.int32, edge.shape, 1)
    edge = jnp.where(lane < 127, edge, 0.0).astype(jnp.bfloat16)
    south = jnp.concatenate([south[:, : HALF - 128], edge], axis=1)
    back_row = lax.broadcasted_iota(jnp.int32, (256, 128), 0)
    back_col = lax.broadcasted_iota(jnp.int32, (256, 128), 1)
    back = jnp.where(back_row + back_col == 254, 1.0, 0.0).astype(jnp.bfloat16)
    for b in range(8):
        if b < 7:
            mirrored = jnp.dot(
                south[:, 128 * (6 - b) : 128 * (8 - b)], back, preferred_element_type=jnp.float32
            )
        else:
            mirrored = jnp.dot(south[:, :128], back[128:], preferred_element_type=jnp.float32)
        here = north[:, 128 * b : 128 * (b + 1)]
        even = (here + mirrored).astype(jnp.bfloat16)
        odd = (here - mirrored).astype(jnp.bfloat16)
        out_ref[:, 0, :, 128 * b : 128 * (b + 1)] = even.reshape(32, 8, 128)
        out_ref[:, 0, :, HALF + 128 * b : HALF + 128 * (b + 1)] = odd.reshape(32, 8, 128)


def fold_coefficients(slots, coeffs):
    row = jnp.arange(256, dtype=jnp.int32)
    j = (row % 8) // 2
    place = jnp.where(j % 2 == 0, row // 8, SPREAD - 1 - row // 8)
    wanted = STRIDE * (SPREAD * j + place)
    hit = jnp.logical_and(
        jnp.repeat(slots, 2)[None, :] == wanted[:, None], row[None, :] % 2 == row[:, None] % 2
    )
    picked = jnp.einsum(
        "pr,src->spc", hit.astype(jnp.bfloat16), coeffs, preferred_element_type=jnp.float32
    ).astype(jnp.bfloat16)
    return pl.pallas_call(
        fold_kernel,
        grid=(2,),
        in_specs=[pl.BlockSpec((1, 256, 2 * HALF), lambda s: (s, 0, 0))],
        out_specs=pl.BlockSpec((32, 1, 8, 2 * HALF), lambda s: (0, s, 0, 0)),
        out_shape=pltpu.HBM((32, 2, 8, 2 * HALF), jnp.bfloat16),
        compiler_params=pltpu.CompilerParams(vmem_limit_bytes=16 * 2**20),
        name="fold",
    )(picked)


def legendre_kernel(
    start_ref, a_ref, ab_ref, cos_ref, weight_ref, seed_ref, level_ref, out_ref, rows_ref
):
    x = cos_ref[...]
    weight = weight_ref[...]
    zero = jnp.zeros((8, 128), jnp.float32)

    for j in range(CHAINS):
        for h in range(2):
            first = table_base(j) + h * half_rows(j)

            def clear(r, carry, first=first):
                rows_ref[pl.ds(pl.multiple_of(8 * (first + r), 8), 8), :] = zero
                return carry

            lax.fori_loop(0, BLOCK_ROWS, clear, 0, unroll=8)

    tracks = CHAINS // 2

    def advance(it, state):
        new_state = []
        for t in range(tracks):
            ja, jb = t, CHAINS - 1 - t
            prev, cur, level = state[t]
            ka, kb = start_ref[ja], start_ref[jb]
            first_len = OWNERS - ka
            in_a = it < first_len
            d = jnp.where(in_a, ka + it, kb + it - first_len)
            k = jnp.where(in_a, ka, kb)
            j = jnp.where(in_a, ja, jb)
            fresh = d == k
            prev = jnp.where(fresh, 0.0, prev)
            cur = jnp.where(fresh, seed_ref[j], cur)
            level = jnp.where(fresh, level_ref[j], level)
            biggest = jnp.maximum(jnp.abs(prev), jnp.abs(cur))
            over = biggest > BIG
            factor = jnp.where(over, SHRINK, 1.0)
            prev = prev * factor
            cur = cur * factor
            level = level + jnp.where(over, 1.0, 0.0)
            scale = weight * jnp.exp2(level * STEP_LOG2)
            coef = j * TABLE + STRIDE * d
            per_half = jnp.where(in_a, half_rows(ja), half_rows(jb))
            first = jnp.where(in_a, table_base(ja), table_base(jb)) + 6 * (d - SPREAD * j)
            for i in range(STRIDE):
                h, within = divmod(i, 6)
                spot = 8 * (first + h * per_half + within)
                rows_ref[pl.ds(pl.multiple_of(spot, 8), 8), :] = cur * scale
                nxt = (a_ref[coef + i] * x) * cur - ab_ref[coef + i] * prev
                prev, cur = cur, nxt
            new_state.append((prev, cur, level))
        return tuple(new_state)

    lax.fori_loop(0, OWNERS + 1, advance, ((zero, zero, zero),) * tracks)

    def pack(block, carry):
        r0 = pl.multiple_of(block * 16, 16)
        for s in range(8):
            v = rows_ref[pl.ds(8 * r0 + s, 16, stride=8), :]
            out_ref[s, pl.ds(r0, 16), :] = v.astype(jnp.bfloat16)
        return carry

    lax.fori_loop(0, TABLE_ROWS // 16, pack, 0, unroll=2)


def legendre_tables(start, a_tab, ab_tab, cosine, weight, seed, level):
    smem = pl.BlockSpec(memory_space=pltpu.SMEM)
    vmem = pl.BlockSpec(memory_space=pltpu.VMEM)
    return pl.pallas_call(
        legendre_kernel,
        in_specs=[smem, smem, smem, vmem, vmem, vmem, vmem],
        out_specs=vmem,
        out_shape=jax.ShapeDtypeStruct((8, TABLE_ROWS, 128), jnp.bfloat16),
        scratch_shapes=[pltpu.VMEM((8 * TABLE_ROWS, 128), jnp.float32)],
        compiler_params=pltpu.CompilerParams(vmem_limit_bytes=28 * 2**20),
        name="legendre",
    )(start, a_tab, ab_tab, cosine, weight, seed, level)


def transform_kernel(table_hbm, x_hbm, out_hbm, table, x_ref, picked, wide, packed, sems):
    loads = []
    for t in range(2):
        span = pl.ds(256 * t, 256)
        copy = pltpu.make_async_copy(
            x_hbm.at[span], x_ref.at[span], sems.at[2 * CHAINS + 2 + t]
        )
        copy.start()
        loads.append(copy)
    copies = []
    for h in range(2):
        for j in range(CHAINS):
            span = pl.ds(table_base(j) + h * half_rows(j), half_rows(j))
            copy = pltpu.make_async_copy(
                table_hbm.at[:, span], table.at[:, span], sems.at[CHAINS * h + j]
            )
            copy.start()
            copies.append(copy)
    row = lax.broadcasted_iota(jnp.int32, (256, 256), 0)
    col = lax.broadcasted_iota(jnp.int32, (256, 256), 1)
    shell = row % 32
    source = (shell // 2) * 16 + (shell % 2) * 8 + (row // 64) * 2 + (row % 64) // 32
    pick = jnp.where(source == col, 1.0, 0.0).astype(jnp.bfloat16)
    for copy in loads:
        copy.wait()
    for t in range(2):
        got = jnp.dot(
            pick, x_ref[256 * t : 256 * (t + 1), :], preferred_element_type=jnp.float32
        ).astype(jnp.bfloat16)
        for j in range(CHAINS):
            mine = got[64 * j : 64 * (j + 1)]
            picked[j, 64 * t : 64 * (t + 1), :] = mine[:, :HALF]
            picked[j, 128 + 64 * t : 128 + 64 * (t + 1), :] = mine[:, HALF:]
    contract = (((1,), (1,)), ((), ()))
    for h in range(2):
        for j in range(CHAINS):
            copies[CHAINS * h + j].wait()
        for j in range(CHAINS):
            gap = BLOCK_ROWS * j
            base = h * 4 * half_rows(0) + j
            if gap:
                wide[pl.ds(base, gap, stride=4), :] = jnp.zeros((gap, 128), jnp.float32)
            for done in range(0, half_rows(j), CHUNK):
                size = min(CHUNK, half_rows(j) - done)
                first = table_base(j) + h * half_rows(j) + done
                rows = jnp.concatenate(
                    [table[s, first : first + size, :] for s in range(8)], axis=1
                )
                got = lax.dot_general(rows, picked[j], contract, preferred_element_type=jnp.float32)
                parity = lax.broadcasted_iota(jnp.int32, (size, 128), 0) % 2
                wide[pl.ds(base + 4 * (gap + done), size, stride=4), :] = jnp.where(
                    parity == 0, got[:, :128], got[:, 128:]
                )
        half = pl.ds(h * 4 * half_rows(0), 4 * half_rows(0))
        packed[half, :] = wide[half, :].astype(jnp.bfloat16)
        copy = pltpu.make_async_copy(packed.at[half], out_hbm.at[half], sems.at[2 * CHAINS + h])
        copy.start()
        copies.append(copy)
    for copy in copies[2 * CHAINS :]:
        copy.wait()


def transform(table, x):
    rows = 8 * half_rows(0)
    hbm = pl.BlockSpec(memory_space=pl.ANY)
    return pl.pallas_call(
        transform_kernel,
        in_specs=[hbm, hbm],
        out_specs=pl.BlockSpec(memory_space=pltpu.HBM),
        out_shape=pltpu.HBM((rows, 128), jnp.bfloat16),
        scratch_shapes=[
            pltpu.VMEM((8, TABLE_ROWS, 128), jnp.bfloat16),
            pltpu.VMEM((512, 2 * HALF), jnp.bfloat16),
            pltpu.VMEM((CHAINS, 256, HALF), jnp.bfloat16),
            pltpu.VMEM((rows, 128), jnp.float32),
            pltpu.VMEM((rows, 128), jnp.bfloat16),
            pltpu.SemaphoreType.DMA((2 * CHAINS + 4,)),
        ],
        compiler_params=pltpu.CompilerParams(vmem_limit_bytes=24 * 2**20),
        name="transform",
    )(
        pltpu.with_memory_space_constraint(table, pltpu.HBM),
        pltpu.with_memory_space_constraint(x, pltpu.HBM),
    )


def degree_fields(wide, i):
    lane = lax.broadcasted_iota(jnp.int32, (PLANE, 128), 1) // 32
    blocks = [[], []]
    for core in range(2):
        for j in range(CHAINS):
            tiles = [[], [], [], []]
            for zh in range(2):
                turned = []
                for z4 in range(4):
                    source = (core * OWNERS + (4 * zh + z4) * PLANE) * 24
                    v = wide[pl.ds(source + 4 * i + j, PLANE, stride=24), :]
                    turned.append(
                        [v] + [pltpu.roll(v, shift=32 * turn, axis=1) for turn in (1, 2, 3)]
                    )
                for part in range(4):
                    tile = turned[0][(0 - part) % 4]
                    for z4 in range(1, 4):
                        tile = jnp.where(lane == z4, turned[z4][(z4 - part) % 4], tile)
                    tiles[part].append(tile)
            for part in range(4):
                blocks[part // 2].append(
                    jnp.concatenate(tiles[part], axis=1).astype(jnp.bfloat16)
                )
    return [jnp.concatenate(rows, axis=0) for rows in blocks]


def cross_kernel(
    who_ref, harm_hbm, own_hbm, other_hbm, out_hbm, harm, wide, basis, out, sems
):
    tracer, owner = who_ref[0], who_ref[1]
    part = OWNERS * 24
    arrivals = []
    for core in range(2):
        span = pl.ds(core * part, part)
        arrivals.append(pltpu.make_async_copy(harm_hbm.at[span], harm.at[span], sems.at[core]))
    for e in range(DEGREES):
        arrivals.append(
            pltpu.make_async_copy(
                own_hbm.at[0, DEGREES * tracer + e], basis.at[tracer, e], sems.at[2 + e]
            )
        )
        arrivals.append(
            pltpu.make_async_copy(
                other_hbm.at[e], basis.at[1 - tracer, e], sems.at[2 + DEGREES + e]
            )
        )
    for copy in arrivals:
        copy.start()
    for core in range(2):
        arrivals[core].wait()
        span = pl.ds(core * part, part)
        wide[span, :] = harm[span, :].astype(jnp.float32)
    tally = jnp.full((1, 512), owner + 1, jnp.int32).astype(jnp.float32)
    factor = 1.0 / jnp.sqrt(2.0 * tally)
    contract = (((1,), (1,)), ((), ()))
    departures = []
    for e0 in range(0, DEGREES, 3):
        group = range(e0, e0 + 3)
        for e in group:
            arrivals[2 + 2 * e].wait()
            arrivals[3 + 2 * e].wait()
        for e in group:
            fields = degree_fields(wide, e)
            lead = lax.dot_general(
                basis[0, e], fields[0], contract, preferred_element_type=jnp.float32
            )
            trail = lax.dot_general(
                fields[1], basis[1, e], contract, preferred_element_type=jnp.float32
            )
            total = jnp.dot(
                lead.astype(jnp.bfloat16),
                trail.astype(jnp.bfloat16),
                preferred_element_type=jnp.float32,
            )
            out[e] = total * factor
        for e in group:
            copy = pltpu.make_async_copy(
                out.at[e], out_hbm.at[0, e], sems.at[2 + 2 * DEGREES + e]
            )
            copy.start()
            departures.append(copy)
    for copy in departures:
        copy.wait()


def cross_spectrum(who, harmonic, bessel, partner):
    hbm = pl.BlockSpec(memory_space=pl.ANY)
    rows = 2 * OWNERS * 24
    return pl.pallas_call(
        cross_kernel,
        in_specs=[pl.BlockSpec(memory_space=pltpu.SMEM), hbm, hbm, hbm],
        out_specs=hbm,
        out_shape=jax.ShapeDtypeStruct((1, DEGREES, 512, 512), jnp.float32),
        scratch_shapes=[
            pltpu.VMEM((rows, 128), jnp.bfloat16),
            pltpu.VMEM((rows, 128), jnp.float32),
            pltpu.VMEM((2, DEGREES, 512, 256), jnp.bfloat16),
            pltpu.VMEM((DEGREES, 512, 512), jnp.float32),
            pltpu.SemaphoreType.DMA((2 + 3 * DEGREES,)),
        ],
        compiler_params=pltpu.CompilerParams(vmem_limit_bytes=32 * 2**20),
        name="cross",
    )(
        who,
        pltpu.with_memory_space_constraint(harmonic, pltpu.HBM),
        pltpu.with_memory_space_constraint(bessel, pltpu.HBM),
        pltpu.with_memory_space_constraint(partner, pltpu.HBM),
    )


def cycle_geometry():
    cycle_number = jnp.arange(1, HALF + 1, dtype=jnp.float32)
    nside_float = jnp.float32(NSIDE)
    polar_cycle = cycle_number < nside_float
    polar_gap = cycle_number * cycle_number / (3.0 * nside_float * nside_float)
    equator_height = 4.0 / 3.0 - 2.0 * cycle_number / (3.0 * nside_float)
    cycle_height = jnp.where(polar_cycle, 1.0 - polar_gap, equator_height)
    height_gap = jnp.where(polar_cycle, polar_gap, 1.0 - equator_height)
    sine_cycle = jnp.sqrt(height_gap * (1.0 + cycle_height))
    pixels = jnp.where(polar_cycle, 4.0 * cycle_number, 4.0 * nside_float)
    weight = jnp.sqrt(jnp.pi * pixels / (3.0 * nside_float * nside_float))
    return (cycle_height, sine_cycle, weight)


def legendre_seed(orders, sine_cycle):
    counter = jnp.arange(1, LMAX + 1, dtype=jnp.float32)
    log_terms = jnp.log1p(-0.5 / counter)
    partial_sum = jnp.sum(
        jnp.where(counter[None, :] <= orders[:, None], log_terms[None, :], 0.0), axis=1
    )
    head = 0.5 * jnp.log((2.0 * orders + 1.0) / (4.0 * jnp.pi)) + 0.5 * partial_sum
    return head[:, None] + orders[:, None] * jnp.log(sine_cycle)[None, :]


def recurrence_tables(orders):
    degree = jnp.arange(1, TABLE + 1, dtype=jnp.float32)[None, :]
    order_col = orders[:, None]
    alpha = jnp.sqrt(
        jnp.maximum(4.0 * degree * degree - 1.0, 1.0)
        / jnp.maximum(degree * degree - order_col * order_col, 1.0)
    )
    below = degree - 1.0
    beta = jnp.sqrt(
        jnp.maximum(below * below - order_col * order_col, 0.0)
        / jnp.maximum(4.0 * below * below - 1.0, 1.0)
    )
    return alpha.reshape(-1), (alpha * beta).reshape(-1)


def per_device(coeffs, bessel, azimuthal_order_slots):
    tracer = lax.axis_index("tracer")
    owner = lax.axis_index("dev")
    place = PLANE * tracer + lax.rem(owner, PLANE)
    plane_groups = [
        [OWNERS * t + PLANE * z + i for t in range(2) for i in range(PLANE)] for z in range(PLANES)
    ]

    away = lax.dynamic_slice_in_dim(bessel[0], (1 - tracer) * 6, 6, 0)
    partner = lax.ppermute(away, "tracer", [(0, 1), (1, 0)])

    folded = fold_coefficients(azimuthal_order_slots, coeffs[0])
    regrouped = lax.all_to_all(
        folded,
        ("tracer", "dev"),
        split_axis=0,
        concat_axis=0,
        tiled=True,
        axis_index_groups=plane_groups,
    )

    start = order_index(jnp.arange(CHAINS, dtype=jnp.int32), place)
    orders = (STRIDE * start).astype(jnp.float32)
    cosine, sine, weight = cycle_geometry()
    seed_log = legendre_seed(orders, sine)
    level = jnp.minimum(jnp.floor(seed_log / (STEP_LN_HIGH + STEP_LN_LOW) + 0.5), 0.0)
    seed = jnp.exp((seed_log - level * STEP_LN_HIGH) - level * STEP_LN_LOW)
    a_tab, ab_tab = recurrence_tables(orders)
    table = legendre_tables(
        start,
        a_tab,
        ab_tab,
        cosine.reshape(8, 128),
        weight.reshape(8, 128),
        seed.reshape(CHAINS, 8, 128),
        level.reshape(CHAINS, 8, 128),
    )

    harmonic = transform(table, regrouped.reshape(512, 2 * HALF))
    by_degree = lax.all_to_all(
        harmonic.reshape(256, 24, 128), ("tracer", "dev"), split_axis=0, concat_axis=0, tiled=True
    )
    who = jnp.stack([tracer, owner]).astype(jnp.int32)
    return cross_spectrum(who, by_degree.reshape(256 * 24, 128), bessel, partner)


def solution(mesh):
    placed = (P("tracer", "dev", None, None), P("tracer", "dev", None, None), P())
    return jax.shard_map(
        per_device,
        mesh=mesh,
        in_specs=placed,
        out_specs=P("tracer", "dev", None, None),
        check_vma=False,
    )
```
